128 devices in a mesh: aa: 32 (over y, x, core), ba: 4 (over z).
Axes of the slice: x: 4, y: 4, z: 4, core: 2. Of those that a mesh axis runs over, the one named last changes fastest.
Arguments:
- table_a: bfloat16 [131072, 768], P('aa'), may hold values from -6 to 6
- table_b: bfloat16 [65536, 768], P(('ba', 'aa')), may hold values from -6 to 6
- pair_a: int32 [32, 4, 32], P('aa', 'ba'), may hold values from 0 to 7, as said below
- pair_b: int32 [32, 4, 32], P('aa', 'ba'), may hold values from 0 to 31, as said below
- pair_count: int32 [32, 4], P('aa', 'ba'), may hold values from 4 to 32, as said below
Outputs:
- log_u: float32 [131072], P('aa')
- log_v: float32 [65536], P(('ba', 'aa'))
The draws below stay inside these ranges and needn't reach their ends.
Inputs may be any that keep to these rules, and one draw needn't show every extreme that they name: `pair_a`: each entry names one of the 8 A blocks of its owner. `pair_b`: each entry names one of the 32 blocks of its B slab; within one list no two slots name the same A block and B block together. `pair_count`: some list is full in every draw.
All inputs are finite; a program needn't handle non-finite values.
Results may differ from the reference program's by a relative error of at most 0.0003.
Values may be sent and summed in bfloat16 or wider, within the bound.
No kernel may reach another device: no remote copies, remote signals or barrier semaphores. Data moves between devices by JAX's collectives and lax.ppermute only.
A program may use at most 128 MiB of HBM per device.

```python
import math
import jax
import jax.numpy as jnp
from jax import lax

D = 768
TILE = 512
ABLK = 8
ITERS = 3
SLOTS = 32
NA = 131072
NB = 65536
N_AA = 32
N_BA = 4


def pair_combos(key):
    keys = jax.random.split(jax.random.fold_in(key, 7), N_AA * N_BA)
    combos = jax.vmap(lambda k: jax.random.permutation(k, ABLK * N_AA)[:SLOTS])(keys)
    return combos.reshape(N_AA, N_BA, SLOTS).astype(jnp.int32)


def draw_pair_a(key, part):
    return pair_combos(key) // N_AA


def draw_pair_b(key, part):
    return pair_combos(key) % N_AA


def draw_pair_count(key, part):
    low = max(1, SLOTS // 8)
    counts = jax.random.randint(jax.random.fold_in(key, 11), (N_AA * N_BA,), low, SLOTS + 1).astype(jnp.int32)
    full = jax.random.randint(jax.random.fold_in(key, 13), (), 0, N_AA * N_BA)
    counts = counts.at[full].set(SLOTS)
    return counts.reshape(N_AA, N_BA).astype(jnp.int32)


def block_levels(key, shape, cuts, low, high):
    loudness = 1.0
    for position, parts in cuts:
        heights = jax.random.uniform(jax.random.fold_in(jax.random.fold_in(key, 6), position), (parts,), jnp.float32, low / len(cuts), high / len(cuts))
        loudness = loudness * jnp.repeat(jnp.exp(heights), shape[position] // parts).reshape((-1,) + (1,) * (len(shape) - 1 - position))
    return loudness


def normal_values(stream_key, dims, deviation, bound, shards=(), kind=jnp.bfloat16):
    result = deviation * jax.random.normal(stream_key, dims, jnp.float32)
    if shards:
        result = result * block_levels(stream_key, dims, shards, -0.22, 0.18)
    return jnp.clip(result, -bound, bound).astype(kind)


def setup_inputs(seed: int = 0) -> dict:
    key_of = jax.random.split(jax.random.key(seed), 6)
    return {
        "table_a": normal_values(key_of[0], (NA, D), 1.0, 6.0, ((0, 32),)),
        "table_b": normal_values(key_of[1], (NB, D), 1.0, 6.0, ((0, 128),)),
        "pair_a": draw_pair_a(jax.random.fold_in(key_of[5], 71), 0),
        "pair_b": draw_pair_b(jax.random.fold_in(key_of[5], 71), 0),
        "pair_count": draw_pair_count(jax.random.fold_in(key_of[5], 71), 0),
    }


def reference(table_a, table_b, pair_a, pair_b, pair_count):
    scale = 2.5 / math.sqrt(D)
    owner_a = jnp.arange(N_AA, dtype=jnp.int32)[:, None, None]
    owner_b = jnp.arange(N_BA, dtype=jnp.int32)[None, :, None]
    glob_a = (owner_a * ABLK + pair_a).reshape(-1).astype(jnp.int32)
    glob_b = (owner_b * N_AA + pair_b).reshape(-1).astype(jnp.int32)
    slot_ids = jnp.arange(SLOTS, dtype=jnp.int32)[None, None, :]
    live = (slot_ids < pair_count[:, :, None]).reshape(-1)

    def make_tile(entry):
        index_a, index_b, alive = entry

        def build(unused):
            block_a = lax.dynamic_slice_in_dim(table_a, (index_a * TILE).astype(jnp.int32), TILE, 0).astype(jnp.float32)
            block_b = lax.dynamic_slice_in_dim(table_b, (index_b * TILE).astype(jnp.int32), TILE, 0).astype(jnp.float32)
            score = lax.dot_general(block_a, block_b, (((1,), (1,)), ((), ())), precision=lax.Precision.HIGHEST)
            return jnp.exp(score * scale).astype(jnp.bfloat16)

        def blank(unused):
            return jnp.zeros((TILE, TILE), jnp.bfloat16)
        return lax.cond(alive, build, blank, 0)
    tiles = lax.map(make_tile, (glob_a, glob_b, live))
    v_blocks = jnp.ones((NB // TILE, TILE), jnp.float32)
    u_blocks = jnp.ones((NA // TILE, TILE), jnp.float32)
    for step in range(ITERS):
        v_round = v_blocks.astype(jnp.bfloat16)
        rows = lax.map(lambda e: jnp.dot(e[0], e[1], preferred_element_type=jnp.float32), (tiles, v_round[glob_b]))
        kernel_a = jax.ops.segment_sum(rows, glob_a, num_segments=NA // TILE)
        u_blocks = 1.0 / (1.0 + kernel_a)
        u_round = u_blocks.astype(jnp.bfloat16)
        cols = lax.map(lambda e: jnp.dot(e[1], e[0], preferred_element_type=jnp.float32), (tiles, u_round[glob_a]))
        kernel_b = jax.ops.segment_sum(cols, glob_b, num_segments=NB // TILE)
        v_blocks = 1.0 / (1.0 + kernel_b)
    return (jnp.log(u_blocks).reshape(-1), jnp.log(v_blocks).reshape(-1))
```

```python
import math

import jax
import jax.numpy as jnp
from jax import lax
from jax.experimental import pallas as pl
from jax.experimental.pallas import tpu as pltpu
from jax.sharding import PartitionSpec as P

TILE = 512
ABLK = 8
ITERS = 3
NY, NX, NC, NZ = 4, 4, 2, 4
NCHIP = NY * NX
SLOTS = 32
CAP = NC * SLOTS
F32 = jnp.float32
BF16 = jnp.bfloat16
VM = pl.BlockSpec(memory_space=pltpu.VMEM)
SM = pl.BlockSpec(memory_space=pltpu.SMEM)
ANY = pl.BlockSpec(memory_space=pl.ANY)


def plan_pairs(lists, pairs, total, tally):
    core = lists[0, 2 * SLOTS + 1]
    for k in range(NCHIP + 1):
        tally[k] = 0

    def scan(body):
        for which in range(NC):
            live = lists[which, 2 * SLOTS]

            def step(s, carry, which=which):
                b = lists[which, SLOTS + s]

                @pl.when((b % NC) == core)
                def _():
                    body(which * ABLK + lists[which, s], b // NC)

                return carry

            lax.fori_loop(0, jnp.minimum(live, SLOTS), step, 0)

    def count(a, b):
        tally[b + 1] = tally[b + 1] + 1

    scan(count)
    for k in range(NCHIP):
        tally[k + 1] = tally[k + 1] + tally[k]

    total[0] = tally[NCHIP]

    def place(a, b):
        spot = tally[b]
        pairs[0, spot] = a
        pairs[1, spot] = b
        tally[b] = spot + 1

    scan(place)


def build_kernel(scale, lists, a_mine, a_other, b_all, store, out, pairs, total, abuf, bbuf, kv, tally, sems):
    plan_pairs(lists, pairs, total, tally)
    core = lists[0, 2 * SLOTS + 1]
    number = total[0]
    kv[...] = jnp.zeros_like(kv)

    def fetch(t, slot):
        a = pairs[0, t]
        row = pl.multiple_of((a % ABLK) * TILE, TILE)

        @pl.when(a // ABLK == core)
        def _():
            pltpu.make_async_copy(a_mine.at[pl.ds(row, TILE)], abuf.at[slot], sems.at[0, slot]).start()

        @pl.when(a // ABLK != core)
        def _():
            pltpu.make_async_copy(a_other.at[pl.ds(row, TILE)], abuf.at[slot], sems.at[0, slot]).start()

        brow = pl.multiple_of(pairs[1, t] * TILE, TILE)
        pltpu.make_async_copy(b_all.at[pl.ds(brow, TILE)], bbuf.at[slot], sems.at[1, slot]).start()

    @pl.when(number > 0)
    def _():
        fetch(0, 0)

    def step(t, carry):
        slot = t % 2

        @pl.when(t + 1 < number)
        def _():
            fetch(t + 1, 1 - slot)

        pltpu.make_async_copy(a_mine.at[pl.ds(0, TILE)], abuf.at[slot], sems.at[0, slot]).wait()
        pltpu.make_async_copy(b_all.at[pl.ds(0, TILE)], bbuf.at[slot], sems.at[1, slot]).wait()
        a = pairs[0, t]
        ones = jnp.ones((16, TILE), BF16)
        rows = 256
        for r in range(0, TILE, rows):
            score = lax.dot_general(
                abuf[slot, pl.ds(r, rows), :], bbuf[slot], (((1,), (1,)), ((), ())), preferred_element_type=F32
            )
            tile = jnp.exp(score * scale).astype(BF16)
            store[t, pl.ds(r, rows), :] = tile
            part = lax.dot_general(ones, tile, (((1,), (1,)), ((), ())), preferred_element_type=F32)
            kv[pl.ds(a, 1), pl.ds(r, rows)] += part[0:1]
        return carry

    lax.fori_loop(0, number, step, 0)
    spread(out, kv[...])


def spread(out, value):
    for k in range(out.shape[0]):
        out[k] = value


def pass_kernel(over_rows, pairs, total, parts, store, out, sums, weight):
    weight[...] = (1.0 / (1.0 + jnp.sum(parts[...], axis=0))).astype(BF16).astype(F32)
    sums[...] = jnp.zeros_like(sums)

    def step(t, carry):
        a = pairs[0, t]
        b = pairs[1, t]
        source, target = (b, a) if over_rows else (a, b)
        row = jnp.broadcast_to(weight[pl.ds(source, 1), :], (16, TILE)).astype(BF16)
        dims = (((1,), (1,)), ((), ())) if over_rows else (((1,), (0,)), ((), ()))
        part = lax.dot_general(row, store[t], dims, preferred_element_type=F32)
        sums[pl.ds(target, 1), :] += part[0:1]
        return carry

    lax.fori_loop(0, total[0], step, 0)
    spread(out, sums[...])


def params(mib=16):
    return pltpu.CompilerParams(vmem_limit_bytes=mib << 20)


def on_device(table_a, table_b, pair_a, pair_b, pair_count):
    scale = 2.5 / math.sqrt(table_a.shape[1])
    width = table_a.shape[1]
    core = lax.axis_index("core")
    swap = [(0, 1), (1, 0)]
    b_all = lax.all_gather(table_b, ("y", "x"), axis=0, tiled=True)
    a_other = lax.ppermute(table_a, "core", swap)
    own = jnp.concatenate(
        [pair_a.reshape(1, -1), pair_b.reshape(1, -1), pair_count.reshape(1, 1), jnp.full((1, 63), core, jnp.int32)],
        axis=1,
    )
    other = lax.ppermute(own, "core", swap)
    first = jnp.where(core == 0, own, other)
    second = jnp.where(core == 0, other, own)
    mark = jnp.arange(128)[None] > 2 * SLOTS
    lists = jnp.where(mark, core, jnp.concatenate([first, second], axis=0)).astype(jnp.int32)

    store, kv, pairs, total = pl.pallas_call(
        lambda *refs: build_kernel(scale, *refs),
        out_shape=(
            pltpu.VMEM((CAP, TILE, TILE), BF16),
            jax.ShapeDtypeStruct((NC * NZ, NC * ABLK, TILE), F32),
            jax.ShapeDtypeStruct((2, CAP), jnp.int32),
            jax.ShapeDtypeStruct((1,), jnp.int32),
        ),
        in_specs=[SM, ANY, ANY, ANY],
        out_specs=(VM, VM, SM, SM),
        scratch_shapes=[
            pltpu.VMEM((2, TILE, width), BF16),
            pltpu.VMEM((2, TILE, width), BF16),
            pltpu.VMEM((NC * ABLK, TILE), F32),
            pltpu.SMEM((NCHIP + 1,), jnp.int32),
            pltpu.SemaphoreType.DMA((2, 2)),
        ],
        compiler_params=params(),
        name="build",
    )(lists, table_a, a_other, b_all)

    def half(over_rows, parts, copies, name):
        return pl.pallas_call(
            lambda *refs: pass_kernel(over_rows, *refs),
            out_shape=jax.ShapeDtypeStruct((copies, NCHIP, TILE), F32),
            in_specs=[SM, SM, VM, VM],
            out_specs=VM,
            scratch_shapes=[pltpu.VMEM((NCHIP, TILE), F32), pltpu.VMEM((NCHIP, TILE), F32)],
            compiler_params=params(),
            name=name,
        )(pairs, total, parts, store)

    for step in range(ITERS):
        if step:
            kv = half(True, ktu_parts, NC * NZ, "rows")
        kv_parts = lax.all_to_all(kv, ("core", "z"), 0, 0, tiled=True)
        ktu = half(False, kv_parts, NCHIP, "columns")
        ktu_parts = lax.all_to_all(ktu, ("y", "x"), 0, 0, tiled=True)
    mine = lax.axis_index("y") * NX + lax.axis_index("x")
    u_sum = lax.dynamic_slice_in_dim(kv_parts, core * ABLK, ABLK, 1)
    v_sum = lax.dynamic_slice_in_dim(ktu_parts, mine, 1, 1)

    def final(parts):
        return jnp.log(1.0 / (1.0 + jnp.sum(parts, axis=0))).reshape(-1)

    return final(u_sum), final(v_sum)


def solution(mesh):
    fine = jax.sharding.Mesh(mesh.devices.reshape(NY, NX, NC, NZ), ("y", "x", "core", "z"))
    a_axes = ("y", "x", "core")
    b_axes = ("z", "y", "x", "core")
    in_specs = (P(a_axes, None), P(b_axes, None), P(a_axes, "z", None), P(a_axes, "z", None), P(a_axes, "z"))
    out_specs = (P(a_axes), P(b_axes))
    return jax.shard_map(on_device, mesh=fine, in_specs=in_specs, out_specs=out_specs, check_vma=False)
```

```python
import math

import jax
import jax.numpy as jnp
from jax import lax
from jax.experimental import pallas as pl
from jax.experimental.pallas import tpu as pltpu
from jax.sharding import PartitionSpec as P

TILE = 512
ABLK = 8
ITERS = 3
NY, NX, NC, NZ = 4, 4, 2, 4
NCHIP = NY * NX
SLOTS = 32
CAP = NC * SLOTS
F32 = jnp.float32
BF16 = jnp.bfloat16
VM = pl.BlockSpec(memory_space=pltpu.VMEM)
SM = pl.BlockSpec(memory_space=pltpu.SMEM)
HB = pl.BlockSpec(memory_space=pltpu.HBM)


ORDER = (
    ((0, 0),),
    ((3, 0), (1, 0), (0, 3), (0, 1)),
    ((2, 0), (3, 3), (1, 3), (3, 1), (1, 1), (0, 2)),
    ((2, 3), (2, 1), (3, 2), (1, 2), (2, 2)),
)


def plan_kernel(lists, place, table, pairs, bounds, tally):
    core, my_y, my_x = place[0], place[1], place[2]
    for k in range(NCHIP + 1):
        tally[k] = 0

    def scan(body):
        for which in range(NC):
            live = lists[which, 2 * SLOTS]

            def step(s, carry, which=which):
                b = lists[which, SLOTS + s]

                @pl.when((b % NC) == core)
                def _():
                    chip = b // NC
                    dy = (chip // NX - my_y + NY) % NY
                    dx = (chip % NX - my_x + NX) % NX
                    code = jnp.where(core == 0, dx * NY + dy, dy * NX + dx)
                    body(which * ABLK + lists[which, s], chip, table[code])

                return carry

            lax.fori_loop(0, jnp.minimum(live, SLOTS), step, 0)

    def count(a, chip, rank):
        tally[rank + 1] = tally[rank + 1] + 1

    scan(count)
    for k in range(NCHIP):
        tally[k + 1] = tally[k + 1] + tally[k]
    for k in range(NCHIP + 1):
        bounds[k] = tally[k]

    def put(a, chip, rank):
        spot = tally[rank]
        pairs[0, spot] = a
        pairs[1, spot] = chip
        pairs[2, spot] = rank
        tally[rank] = spot + 1

    scan(put)


def alloc_kernel(pairs, bounds, place, store):
    pass


def build_kernel(scale, first, blocks, last, pairs, bounds, place, a_mine, a_other, *refs):
    b_refs, (_, kv_in, store, out), (kv, abuf, bbuf, sems) = refs[:blocks], refs[blocks : blocks + 4], refs[blocks + 4 :]
    core = place[0]
    low, high = bounds[first], bounds[first + blocks]
    kv[...] = kv_in[...]

    def fetch(t, slot):
        a = pairs[0, t]
        row = pl.multiple_of((a % ABLK) * TILE, TILE)

        @pl.when(a // ABLK == core)
        def _():
            pltpu.make_async_copy(a_mine.at[pl.ds(row, TILE)], abuf.at[slot], sems.at[0, slot]).start()

        @pl.when(a // ABLK != core)
        def _():
            pltpu.make_async_copy(a_other.at[pl.ds(row, TILE)], abuf.at[slot], sems.at[0, slot]).start()

        for k in range(blocks):

            @pl.when(pairs[2, t] == first + k)
            def _():
                pltpu.make_async_copy(b_refs[k], bbuf.at[slot], sems.at[1, slot]).start()

    @pl.when(high > low)
    def _():
        fetch(low, 0)

    def step(t, carry):
        slot = (t - low) % 2

        @pl.when(t + 1 < high)
        def _():
            fetch(t + 1, 1 - slot)

        pltpu.make_async_copy(a_mine.at[pl.ds(0, TILE)], abuf.at[slot], sems.at[0, slot]).wait()
        pltpu.make_async_copy(b_refs[0], bbuf.at[slot], sems.at[1, slot]).wait()
        a = pairs[0, t]
        ones = jnp.ones((16, TILE), BF16)
        rows = 256
        for r in range(0, TILE, rows):
            score = lax.dot_general(
                abuf[slot, pl.ds(r, rows), :], bbuf[slot], (((1,), (1,)), ((), ())), preferred_element_type=F32
            )
            tile = jnp.exp(score * scale).astype(BF16)
            store[t, pl.ds(r, rows), :] = tile
            part = lax.dot_general(ones, tile, (((1,), (1,)), ((), ())), preferred_element_type=F32)
            kv[pl.ds(a, 1), pl.ds(r, rows)] += part[0:1]
        return carry

    lax.fori_loop(low, high, step, 0)
    if last:
        spread(out, kv[...])
    else:
        out[...] = kv[...]


def spread(out, value):
    for k in range(out.shape[0]):
        out[k] = value


def pass_kernel(over_rows, pairs, bounds, place, parts, store, out, _, sums, weight):
    weight[...] = (1.0 / (1.0 + jnp.sum(parts[...], axis=0))).astype(BF16).astype(F32)
    sums[...] = jnp.zeros_like(sums)

    def step(t, carry):
        a = pairs[0, t]
        b = pairs[1, t]
        source, target = (b, a) if over_rows else (a, b)
        row = jnp.broadcast_to(weight[pl.ds(source, 1), :], (16, TILE)).astype(BF16)
        dims = (((1,), (1,)), ((), ())) if over_rows else (((1,), (0,)), ((), ()))
        part = lax.dot_general(row, store[t], dims, preferred_element_type=F32)
        sums[pl.ds(target, 1), :] += part[0:1]
        return carry

    lax.fori_loop(0, bounds[NCHIP], step, 0)
    spread(out, sums[...])


def params(mib=16):
    return pltpu.CompilerParams(vmem_limit_bytes=mib << 20)


def moves(first, shift):
    pairs = []
    for y in range(NY):
        for x in range(NX):
            for c in range(NC):
                dy, dx = (0, shift) if (c == 0) == first else (shift, 0)
                there = ((y + dy) % NY * NX + (x + dx) % NX) * NC + c
                pairs.append(((y * NX + x) * NC + c, there))
    return pairs


def gather_groups(own):
    def go(block, first, shift):
        moved = lax.ppermute(block, ("y", "x", "core"), moves(first, shift))
        return pltpu.with_memory_space_constraint(moved, pltpu.HBM)

    left, right = go(own, True, 1), go(own, True, -1)
    down, up = go(own, False, 1), go(own, False, -1)
    left_down, left_up = go(left, False, 1), go(left, False, -1)
    right_down, right_up = go(right, False, 1), go(right, False, -1)
    first_two, second_two = go(left, True, 1), go(down, False, 1)
    two_down, two_up = go(first_two, False, 1), go(first_two, False, -1)
    left_two, right_two, both_two = go(left_up, False, -1), go(right_down, False, 1), go(two_up, False, -1)
    return (
        (own,),
        (left, right, down, up),
        (first_two, left_down, right_down, left_up, right_up, second_two),
        (two_down, two_up, left_two, right_two, both_two),
    )


def on_device(table_a, table_b, pair_a, pair_b, pair_count):
    width = table_a.shape[1]
    scale = 2.5 / math.sqrt(width)
    core = lax.axis_index("core")
    swap = [(0, 1), (1, 0)]
    own = jnp.concatenate(
        [pair_a.reshape(1, -1), pair_b.reshape(1, -1), pair_count.reshape(1, 1), jnp.zeros((1, 63), jnp.int32)], axis=1
    )
    other = lax.ppermute(own, "core", swap)
    a_other = lax.ppermute(table_a, "core", swap)
    lists = jnp.where(core == 0, jnp.concatenate([own, other]), jnp.concatenate([other, own]))
    place = jnp.stack([core, lax.axis_index("y"), lax.axis_index("x")]).astype(jnp.int32)
    table = [0] * NCHIP
    for rank, (f, s) in enumerate(sum(ORDER, ())):
        table[f * NY + s] = rank
    groups = gather_groups(table_b)

    pairs, bounds = pl.pallas_call(
        plan_kernel,
        out_shape=(jax.ShapeDtypeStruct((3, CAP), jnp.int32), jax.ShapeDtypeStruct((NCHIP + 1,), jnp.int32)),
        in_specs=[SM, SM, SM],
        out_specs=(SM, SM),
        scratch_shapes=[pltpu.SMEM((NCHIP + 1,), jnp.int32)],
        compiler_params=params(1),
        name="plan",
    )(lists, place, jnp.array(table, jnp.int32))

    store = pl.pallas_call(
        alloc_kernel,
        out_shape=pltpu.VMEM((CAP, TILE, TILE), BF16),
        in_specs=[SM, SM, SM],
        out_specs=VM,
        compiler_params=params(),
        name="alloc",
    )(pairs, bounds, place)
    kv = jnp.zeros((NC * ABLK, TILE), F32)
    first = 0
    for group in groups:
        blocks = len(group)
        last = first + blocks == NCHIP
        shape = (NC * NZ, NC * ABLK, TILE) if last else (NC * ABLK, TILE)
        share = 2 * blocks
        store, kv = pl.pallas_call(
            lambda *refs, first=first, blocks=blocks, last=last: build_kernel(scale, first, blocks, last, *refs),
            out_shape=(pltpu.VMEM((CAP, TILE, TILE), BF16), jax.ShapeDtypeStruct(shape, F32)),
            in_specs=[SM, SM, SM] + [HB] * (2 + blocks) + [VM, VM],
            out_specs=(VM, VM),
            scratch_shapes=[
                pltpu.VMEM((NC * ABLK, TILE), F32),
                pltpu.VMEM((2, TILE, width), BF16),
                pltpu.VMEM((2, TILE, width), BF16),
                pltpu.SemaphoreType.DMA((2, 2)),
            ],
            input_output_aliases={5 + blocks: 0},
            cost_estimate=pl.CostEstimate(
                flops=share * 2 * TILE * TILE * width,
                transcendentals=share * TILE * TILE,
                bytes_accessed=share * 2 * TILE * width * 2,
            ),
            compiler_params=params(),
            name="build",
        )(pairs, bounds, place, table_a, a_other, *group, store, kv)
        first += blocks
    def half(over_rows, parts, copies, name, store):
        return pl.pallas_call(
            lambda *refs: pass_kernel(over_rows, *refs),
            out_shape=(jax.ShapeDtypeStruct((copies, NCHIP, TILE), F32), pltpu.VMEM((CAP, TILE, TILE), BF16)),
            in_specs=[SM, SM, SM, VM, VM],
            out_specs=(VM, VM),
            input_output_aliases={4: 1},
            scratch_shapes=[pltpu.VMEM((NCHIP, TILE), F32), pltpu.VMEM((NCHIP, TILE), F32)],
            compiler_params=params(),
            name=name,
        )(pairs, bounds, place, parts, store)

    for step in range(ITERS):
        if step:
            kv, store = half(True, ktu_parts, NC * NZ, "rows", store)
        kv_parts = lax.all_to_all(kv, ("core", "z"), 0, 0, tiled=True)
        ktu, store = half(False, kv_parts, NCHIP, "columns", store)
        ktu_parts = lax.all_to_all(ktu, ("y", "x"), 0, 0, tiled=True)
    mine = lax.axis_index("y") * NX + lax.axis_index("x")
    u_sum = lax.dynamic_slice_in_dim(kv_parts, core * ABLK, ABLK, 1)
    v_sum = lax.dynamic_slice_in_dim(ktu_parts, mine, 1, 1)

    def final(parts):
        return jnp.log(1.0 / (1.0 + jnp.sum(parts, axis=0))).reshape(-1)

    return final(u_sum), final(v_sum)


def solution(mesh):
    fine = jax.sharding.Mesh(mesh.devices.reshape(NY, NX, NC, NZ), ("y", "x", "core", "z"))
    a_axes = ("y", "x", "core")
    b_axes = ("z", "y", "x", "core")
    in_specs = (P(a_axes, None), P(b_axes, None), P(a_axes, "z", None), P(a_axes, "z", None), P(a_axes, "z"))
    out_specs = (P(a_axes), P(b_axes))
    return jax.shard_map(on_device, mesh=fine, in_specs=in_specs, out_specs=out_specs, check_vma=False)
```

```python
import math

import jax
import jax.numpy as jnp
from jax import lax
from jax.experimental import pallas as pl
from jax.experimental.pallas import tpu as pltpu
from jax.sharding import PartitionSpec as P

TILE = 512
ABLK = 8
ITERS = 3
BUILD_STEP = 2
BUFFERS = 4
ROW_STEP = 4
COLUMN_STEP = 8
NY, NX, NC, NZ = 4, 4, 2, 4
NCHIP = NY * NX
SLOTS = 32
CAP = NC * SLOTS
F32 = jnp.float32
BF16 = jnp.bfloat16
VM = pl.BlockSpec(memory_space=pltpu.VMEM)
SM = pl.BlockSpec(memory_space=pltpu.SMEM)
ANY = pl.BlockSpec(memory_space=pl.ANY)
HB = pl.BlockSpec(memory_space=pltpu.HBM)


ORDER = (
    ((0, 0),),
    ((3, 0), (1, 0), (0, 3), (0, 1)),
    ((2, 0), (3, 3), (1, 3), (3, 1), (1, 1)),
    ((0, 2), (2, 3), (2, 1), (3, 2), (1, 2)),
    ((2, 2),),
)


def plan_kernel(lists, place, table, pairs, bounds, tally):
    core, my_y, my_x = place[0], place[1], place[2]
    for k in range(NCHIP + 1):
        tally[k] = 0

    def scan(body):
        for which in range(NC):
            live = lists[which, 2 * SLOTS]

            def step(s, carry, which=which):
                b = lists[which, SLOTS + s]

                @pl.when((b % NC) == core)
                def _():
                    chip = b // NC
                    dy = (chip // NX - my_y + NY) % NY
                    dx = (chip % NX - my_x + NX) % NX
                    code = jnp.where(core == 0, dx * NY + dy, dy * NX + dx)
                    body(which * ABLK + lists[which, s], chip, table[code])

                return carry

            lax.fori_loop(0, jnp.minimum(live, SLOTS), step, 0)

    def count(a, chip, rank):
        tally[rank + 1] = tally[rank + 1] + 1

    scan(count)
    for k in range(NCHIP):
        tally[k + 1] = tally[k + 1] + tally[k]
    for k in range(NCHIP + 1):
        bounds[k] = tally[k]

    def put(a, chip, rank):
        spot = tally[rank]
        pairs[0, spot] = a
        pairs[1, spot] = chip
        pairs[2, spot] = rank
        tally[rank] = spot + 1

    scan(put)


def room_kernel(pairs, bounds, place, store):
    pass


def build_kernel(scale, first, blocks, last, pairs, bounds, place, a_mine, a_other, *refs):
    b_refs, (_, kv_in, store, out), scratch = refs[:blocks], refs[blocks : blocks + 4], refs[blocks + 4 :]
    kv, abuf, bbuf, a_sems, b_sems = scratch
    core = place[0]
    low, high = bounds[first], bounds[first + blocks]
    ahead = BUFFERS - BUILD_STEP

    def fetch(t):
        @pl.when(t < high)
        def _():
            a = pairs[0, t]
            slot = (t - low) % BUFFERS
            row = pl.multiple_of((a % ABLK) * TILE, TILE)

            @pl.when(a // ABLK == core)
            def _():
                pltpu.make_async_copy(a_mine.at[pl.ds(row, TILE)], abuf.at[slot], a_sems.at[slot]).start()

            @pl.when(a // ABLK != core)
            def _():
                pltpu.make_async_copy(a_other.at[pl.ds(row, TILE)], abuf.at[slot], a_sems.at[slot]).start()

    loads = [pltpu.make_async_copy(b_refs[k], bbuf.at[k], b_sems.at[k]) for k in range(blocks)]
    for load in loads:
        load.start()
    for k in range(ahead):
        fetch(low + k)
    kv[...] = kv_in[...]
    ones = jnp.ones((16, TILE), BF16)
    for load in loads:
        load.wait()

    def step(c, carry):
        base = low + c * BUILD_STEP
        for k in range(BUILD_STEP):
            fetch(base + ahead + k)
        for k in range(BUILD_STEP):

            @pl.when(base + k < high)
            def _(k=k):
                slot = (base + k - low) % BUFFERS
                pltpu.make_async_copy(a_mine.at[pl.ds(0, TILE)], abuf.at[slot], a_sems.at[slot]).wait()

        sums = []
        for k in range(BUILD_STEP):
            t = jnp.minimum(base + k, high - 1)
            block_a, block_b = abuf[(t - low) % BUFFERS], bbuf[pairs[2, t] - first]
            score = lax.dot_general(block_a, block_b, (((1,), (1,)), ((), ())), preferred_element_type=F32)
            tile = jnp.exp(score * scale).astype(BF16)
            store[t] = tile
            part = lax.dot_general(ones, tile, (((1,), (1,)), ((), ())), preferred_element_type=F32)
            sums.append((pairs[0, t], jnp.where(base + k < high, part[0:1], 0.0)))
        for a, part in sums:
            kv[pl.ds(a, 1), :] += part
        return carry

    lax.fori_loop(0, (high - low + BUILD_STEP - 1) // BUILD_STEP, step, 0)
    if last:
        spread(out, kv[...])
    else:
        out[...] = kv[...]


def spread(out, value):
    for k in range(out.shape[0]):
        out[k] = value


def pass_kernel(over_rows, last, pairs, bounds, place, parts, store, out, *refs):
    sums, weight = refs[-2:]
    scaling = 1.0 / (1.0 + jnp.sum(parts[...], axis=0))
    weight[...] = scaling.astype(BF16).astype(F32)
    if last:
        refs[0][...] = jnp.log(jnp.where(place[0] == 0, scaling[:ABLK], scaling[ABLK:]))
    sums[...] = jnp.zeros_like(sums)
    number = bounds[NCHIP]
    size = ROW_STEP if over_rows else COLUMN_STEP
    dims = (((1,), (1,)), ((), ())) if over_rows else (((1,), (0,)), ((), ()))

    def step(c, carry):
        found = []
        for k in range(size):
            t = c * size + k
            safe = jnp.minimum(t, number - 1)
            a = pairs[0, safe]
            b = pairs[1, safe]
            source, target = (b, a) if over_rows else (a, b)
            row = jnp.where(t < number, weight[pl.ds(source, 1), :], 0.0)
            row = jnp.broadcast_to(row, (16, TILE)).astype(BF16)
            found.append((target, lax.dot_general(row, store[safe], dims, preferred_element_type=F32)))
        for target, part in found:
            sums[pl.ds(target, 1), :] += part[0:1]
        return carry

    lax.fori_loop(0, (number + size - 1) // size, step, 0)
    if last:
        out[...] = sums[...]
    else:
        spread(out, sums[...])


def params(mib=16):
    return pltpu.CompilerParams(vmem_limit_bytes=mib << 20)


def moves(first, shift):
    pairs = []
    for y in range(NY):
        for x in range(NX):
            for c in range(NC):
                dy, dx = (0, shift) if (c == 0) == first else (shift, 0)
                there = ((y + dy) % NY * NX + (x + dx) % NX) * NC + c
                pairs.append(((y * NX + x) * NC + c, there))
    return pairs


def go(block, first, shift):
    return lax.ppermute(block, ("y", "x", "core"), moves(first, shift))


def on_device(table_a, table_b, pair_a, pair_b, pair_count):
    width = table_a.shape[1]
    scale = 2.5 / math.sqrt(width)
    core = lax.axis_index("core")
    swap = [(0, 1), (1, 0)]
    own = jnp.concatenate(
        [pair_a.reshape(1, -1), pair_b.reshape(1, -1), pair_count.reshape(1, 1), jnp.zeros((1, 63), jnp.int32)], axis=1
    )
    other = lax.ppermute(own, "core", swap)
    a_other = lax.ppermute(table_a, "core", swap)
    lists = jnp.where(core == 0, jnp.concatenate([own, other]), jnp.concatenate([other, own]))
    place = jnp.stack([core, lax.axis_index("y"), lax.axis_index("x")]).astype(jnp.int32)
    table = [0] * NCHIP
    for rank, (f, s) in enumerate(sum(ORDER, ())):
        table[f * NY + s] = rank
    left, right = go(table_b, True, 1), go(table_b, True, -1)
    down, up = go(table_b, False, 1), go(table_b, False, -1)

    pairs, bounds = pl.pallas_call(
        plan_kernel,
        out_shape=(jax.ShapeDtypeStruct((3, CAP), jnp.int32), jax.ShapeDtypeStruct((NCHIP + 1,), jnp.int32)),
        in_specs=[SM, SM, SM],
        out_specs=(SM, SM),
        scratch_shapes=[pltpu.SMEM((NCHIP + 1,), jnp.int32)],
        compiler_params=params(1),
        name="plan",
    )(lists, place, jnp.array(table, jnp.int32))

    store = pl.pallas_call(
        room_kernel,
        out_shape=pltpu.VMEM((CAP, TILE, TILE), BF16),
        in_specs=[SM, SM, SM],
        out_specs=VM,
        compiler_params=params(),
        name="room",
    )(pairs, bounds, place)

    def build(first, group, store, kv):
        blocks = len(group)
        last = first + blocks == NCHIP
        shape = (NC * NZ, NC * ABLK, TILE) if last else (NC * ABLK, TILE)
        share = 2 * blocks
        return pl.pallas_call(
            lambda *refs: build_kernel(scale, first, blocks, last, *refs),
            out_shape=(pltpu.VMEM((CAP, TILE, TILE), BF16), jax.ShapeDtypeStruct(shape, F32)),
            in_specs=[SM, SM, SM, HB, HB] + [ANY] * blocks + [VM, VM],
            out_specs=(VM, VM),
            scratch_shapes=[
                pltpu.VMEM((NC * ABLK, TILE), F32),
                pltpu.VMEM((BUFFERS, TILE, width), BF16),
                pltpu.VMEM((blocks, TILE, width), BF16),
                pltpu.SemaphoreType.DMA((BUFFERS,)),
                pltpu.SemaphoreType.DMA((blocks,)),
            ],
            input_output_aliases={5 + blocks: 0},
            cost_estimate=pl.CostEstimate(
                flops=share * 2 * TILE * TILE * width,
                transcendentals=share * TILE * TILE,
                bytes_accessed=share * 2 * TILE * width * 2,
            ),
            compiler_params=params(),
            name="build",
        )(pairs, bounds, place, table_a, a_other, *group, store, kv)

    kv = jnp.zeros((NC * ABLK, TILE), F32)
    store, kv = build(0, (table_b,), store, kv)
    left, right, down, up, kv = lax.optimization_barrier((left, right, down, up, kv))
    near = (left, right, down, up)
    first_two = go(right, True, -1)
    left_down, right_down = go(left, False, 1), go(right, False, 1)
    left_up, right_up = go(left, False, -1), go(right, False, -1)
    store, kv = build(1, near, store, kv)
    middle = (first_two, left_down, right_down, left_up, right_up)
    *middle, down, kv = lax.optimization_barrier((*middle, down, kv))
    first_two, left_down, right_down, left_up, right_up = middle
    two_up, two_down = go(first_two, False, -1), go(first_two, False, 1)
    left_two, right_two, second_two = go(left_up, False, -1), go(right_down, False, 1), go(down, False, 1)
    store, kv = build(5, middle, store, kv)
    two_up, kv = lax.optimization_barrier((two_up, kv))
    both_two = go(two_up, False, -1)
    store, kv = build(10, (second_two, two_down, two_up, left_two, right_two), store, kv)
    store, kv = build(15, (both_two,), store, kv)

    def half(over_rows, parts, copies, store):
        last = copies == 0
        sums = jax.ShapeDtypeStruct((NCHIP, TILE) if last else (copies, NCHIP, TILE), F32)
        logs = jax.ShapeDtypeStruct((ABLK, TILE), F32)
        return pl.pallas_call(
            lambda *refs: pass_kernel(over_rows, last, *refs),
            out_shape=(sums, logs if last else pltpu.VMEM((CAP, TILE, TILE), BF16)),
            in_specs=[SM, SM, SM, VM, VM],
            out_specs=(VM, VM),
            scratch_shapes=[pltpu.VMEM((NCHIP, TILE), F32), pltpu.VMEM((NCHIP, TILE), F32)],
            input_output_aliases={} if last else {4: 1},
            compiler_params=params(),
            name="rows" if over_rows else "columns",
        )(pairs, bounds, place, parts, store)

    for step in range(ITERS):
        if step:
            kv, store = half(True, ktu_parts, NC * NZ, store)
        kv_parts = lax.all_to_all(kv, ("core", "z"), 0, 0, tiled=True)
        if step < ITERS - 1:
            ktu, store = half(False, kv_parts, NCHIP, store)
            ktu_parts = lax.all_to_all(ktu, ("y", "x"), 0, 0, tiled=True)
    ktu, log_u = half(False, kv_parts, 0, store)
    mine = lax.all_to_all(ktu, ("y", "x"), 0, 0, tiled=True)
    log_v = jnp.log(1.0 / (1.0 + jnp.sum(mine, axis=0)))
    return log_u.reshape(-1), log_v


def solution(mesh):
    fine = jax.sharding.Mesh(mesh.devices.reshape(NY, NX, NC, NZ), ("y", "x", "core", "z"))
    a_axes = ("y", "x", "core")
    b_axes = ("z", "y", "x", "core")
    in_specs = (P(a_axes, None), P(b_axes, None), P(a_axes, "z", None), P(a_axes, "z", None), P(a_axes, "z"))
    out_specs = (P(a_axes), P(b_axes))
    return jax.shard_map(on_device, mesh=fine, in_specs=in_specs, out_specs=out_specs, check_vma=False)
```

```python
import math

import jax
import jax.numpy as jnp
from jax import lax
from jax.experimental import pallas as pl
from jax.experimental.pallas import tpu as pltpu
from jax.sharding import PartitionSpec as P

TILE = 512
ABLK = 8
ITERS = 3
LANES = 128
BUILD_STEP = 2
BUFFERS = 4
ROW_STEP = 4
COLUMN_STEP = 8
NY, NX, NC, NZ = 4, 4, 2, 4
NCHIP = NY * NX
SLOTS = 32
CAP = NC * SLOTS
F32 = jnp.float32
BF16 = jnp.bfloat16
VM = pl.BlockSpec(memory_space=pltpu.VMEM)
SM = pl.BlockSpec(memory_space=pltpu.SMEM)
ANY = pl.BlockSpec(memory_space=pl.ANY)
HB = pl.BlockSpec(memory_space=pltpu.HBM)


ORDER = (
    ((0, 0),),
    ((3, 0), (1, 0), (0, 3), (0, 1)),
    ((2, 0), (3, 3), (1, 3), (3, 1), (1, 1)),
    ((0, 2), (2, 3), (2, 1), (3, 2), (1, 2)),
    ((2, 2),),
)


def plan_kernel(lists, place, table, pairs, bounds, tally):
    core, my_y, my_x = place[0], place[1], place[2]
    for k in range(NCHIP + 1):
        tally[k] = 0

    def scan(body):
        for which in range(NC):
            live = lists[which, 2 * SLOTS]

            def step(s, carry, which=which):
                b = lists[which, SLOTS + s]

                @pl.when((b % NC) == core)
                def _():
                    chip = b // NC
                    dy = (chip // NX - my_y + NY) % NY
                    dx = (chip % NX - my_x + NX) % NX
                    code = jnp.where(core == 0, dx * NY + dy, dy * NX + dx)
                    body(which * ABLK + lists[which, s], chip, table[code])

                return carry

            lax.fori_loop(0, jnp.minimum(live, SLOTS), step, 0)

    def count(a, chip, rank):
        tally[rank + 1] = tally[rank + 1] + 1

    scan(count)
    for k in range(NCHIP):
        tally[k + 1] = tally[k + 1] + tally[k]
    for k in range(NCHIP + 1):
        bounds[k] = tally[k]

    def put(a, chip, rank):
        spot = tally[rank]
        pairs[0, spot] = a
        pairs[1, spot] = chip
        pairs[2, spot] = rank
        tally[rank] = spot + 1

    scan(put)


def room_kernel(pairs, bounds, place, store):
    pass


def build_kernel(scale, first, blocks, last, pairs, bounds, place, a_mine, a_other, *refs):
    b_refs, (_, kv_in, store, out), scratch = refs[:blocks], refs[blocks : blocks + 4], refs[blocks + 4 :]
    kv, abuf, bbuf, a_sems, b_sems = scratch
    core = place[0]
    low, high = bounds[first], bounds[first + blocks]
    ahead = BUFFERS - BUILD_STEP

    def fetch(t):
        @pl.when(t < high)
        def _():
            a = pairs[0, t]
            slot = (t - low) % BUFFERS
            row = pl.multiple_of((a % ABLK) * TILE, TILE)

            @pl.when(a // ABLK == core)
            def _():
                pltpu.make_async_copy(a_mine.at[pl.ds(row, TILE)], abuf.at[slot], a_sems.at[slot]).start()

            @pl.when(a // ABLK != core)
            def _():
                pltpu.make_async_copy(a_other.at[pl.ds(row, TILE)], abuf.at[slot], a_sems.at[slot]).start()

    loads = [pltpu.make_async_copy(b_refs[k], bbuf.at[k], b_sems.at[k]) for k in range(blocks)]
    for load in loads:
        load.start()
    for k in range(ahead):
        fetch(low + k)
    kv[...] = kv_in[...]
    ones = jnp.ones((16, TILE), BF16)
    for load in loads:
        load.wait()

    def step(c, carry):
        base = low + c * BUILD_STEP
        for k in range(BUILD_STEP):
            fetch(base + ahead + k)
        for k in range(BUILD_STEP):

            @pl.when(base + k < high)
            def _(k=k):
                slot = (base + k - low) % BUFFERS
                pltpu.make_async_copy(a_mine.at[pl.ds(0, TILE)], abuf.at[slot], a_sems.at[slot]).wait()

        sums = []
        for k in range(BUILD_STEP):
            t = jnp.minimum(base + k, high - 1)
            block_a, block_b = abuf[(t - low) % BUFFERS], bbuf[pairs[2, t] - first]
            score = lax.dot_general(block_a, block_b, (((1,), (1,)), ((), ())), preferred_element_type=F32)
            tile = jnp.exp(score * scale).astype(BF16)
            store[t] = tile
            part = lax.dot_general(ones, tile, (((1,), (1,)), ((), ())), preferred_element_type=F32)
            sums.append((pairs[0, t], jnp.where(base + k < high, part[0:1], 0.0)))
        for a, part in sums:
            kv[pl.ds(a, 1), :] += part
        return carry

    lax.fori_loop(0, (high - low + BUILD_STEP - 1) // BUILD_STEP, step, 0)
    if last:
        spread(out, kv[...])
    else:
        out[...] = kv[...]


def spread(out, value):
    for k in range(out.shape[0]):
        out[k] = value


def pass_kernel(over_rows, last, pairs, bounds, place, parts, store, out, *refs):
    sums, weight = refs[-2:]
    scaling = 1.0 / (1.0 + jnp.sum(parts[...], axis=0))
    weight[...] = scaling.astype(BF16).astype(F32)
    if last:
        logs = jnp.log(jnp.where(place[0] == 0, scaling[:ABLK], scaling[ABLK:]))
        for k in range(ABLK):
            for q in range(TILE // LANES):
                refs[0][pl.ds(k * (TILE // LANES) + q, 1), :] = logs[k : k + 1, q * LANES : (q + 1) * LANES]
    sums[...] = jnp.zeros_like(sums)
    number = bounds[NCHIP]
    size = ROW_STEP if over_rows else COLUMN_STEP
    dims = (((1,), (1,)), ((), ())) if over_rows else (((1,), (0,)), ((), ()))

    def step(c, carry):
        found = []
        for k in range(size):
            t = c * size + k
            safe = jnp.minimum(t, number - 1)
            a = pairs[0, safe]
            b = pairs[1, safe]
            source, target = (b, a) if over_rows else (a, b)
            row = jnp.where(t < number, weight[pl.ds(source, 1), :], 0.0)
            row = jnp.broadcast_to(row, (16, TILE)).astype(BF16)
            found.append((target, lax.dot_general(row, store[safe], dims, preferred_element_type=F32)))
        for target, part in found:
            sums[pl.ds(target, 1), :] += part[0:1]
        return carry

    lax.fori_loop(0, (number + size - 1) // size, step, 0)
    if last:
        for q in range(TILE // LANES):
            out[:, q, :] = sums[:, q * LANES : (q + 1) * LANES]
    else:
        spread(out, sums[...])


def params(mib=16):
    return pltpu.CompilerParams(vmem_limit_bytes=mib << 20)


def moves(first, shift):
    pairs = []
    for y in range(NY):
        for x in range(NX):
            for c in range(NC):
                dy, dx = (0, shift) if (c == 0) == first else (shift, 0)
                there = ((y + dy) % NY * NX + (x + dx) % NX) * NC + c
                pairs.append(((y * NX + x) * NC + c, there))
    return pairs


def go(block, first, shift):
    return lax.ppermute(block, ("y", "x", "core"), moves(first, shift))


def on_device(table_a, table_b, pair_a, pair_b, pair_count):
    width = table_a.shape[1]
    scale = 2.5 / math.sqrt(width)
    core = lax.axis_index("core")
    swap = [(0, 1), (1, 0)]
    own = jnp.concatenate(
        [pair_a.reshape(1, -1), pair_b.reshape(1, -1), pair_count.reshape(1, 1), jnp.zeros((1, 63), jnp.int32)], axis=1
    )
    a_other = lax.ppermute(table_a, "core", swap)
    own, a_other = lax.optimization_barrier((own, a_other))
    other = lax.ppermute(own, "core", swap)
    lists = jnp.where(core == 0, jnp.concatenate([own, other]), jnp.concatenate([other, own]))
    place = jnp.stack([core, lax.axis_index("y"), lax.axis_index("x")]).astype(jnp.int32)
    table = [0] * NCHIP
    for rank, (f, s) in enumerate(sum(ORDER, ())):
        table[f * NY + s] = rank
    left, right = go(table_b, True, 1), go(table_b, True, -1)
    down, up = go(table_b, False, 1), go(table_b, False, -1)

    pairs, bounds = pl.pallas_call(
        plan_kernel,
        out_shape=(jax.ShapeDtypeStruct((3, CAP), jnp.int32), jax.ShapeDtypeStruct((NCHIP + 1,), jnp.int32)),
        in_specs=[SM, SM, SM],
        out_specs=(SM, SM),
        scratch_shapes=[pltpu.SMEM((NCHIP + 1,), jnp.int32)],
        compiler_params=params(1),
        name="plan",
    )(lists, place, jnp.array(table, jnp.int32))

    store = pl.pallas_call(
        room_kernel,
        out_shape=pltpu.VMEM((CAP, TILE, TILE), BF16),
        in_specs=[SM, SM, SM],
        out_specs=VM,
        compiler_params=params(),
        name="room",
    )(pairs, bounds, place)

    def build(first, group, store, kv):
        blocks = len(group)
        last = first + blocks == NCHIP
        shape = (NC * NZ, NC * ABLK, TILE) if last else (NC * ABLK, TILE)
        share = 2 * blocks
        return pl.pallas_call(
            lambda *refs: build_kernel(scale, first, blocks, last, *refs),
            out_shape=(pltpu.VMEM((CAP, TILE, TILE), BF16), jax.ShapeDtypeStruct(shape, F32)),
            in_specs=[SM, SM, SM, HB, HB] + [ANY] * blocks + [VM, VM],
            out_specs=(VM, VM),
            scratch_shapes=[
                pltpu.VMEM((NC * ABLK, TILE), F32),
                pltpu.VMEM((BUFFERS, TILE, width), BF16),
                pltpu.VMEM((blocks, TILE, width), BF16),
                pltpu.SemaphoreType.DMA((BUFFERS,)),
                pltpu.SemaphoreType.DMA((blocks,)),
            ],
            input_output_aliases={5 + blocks: 0},
            cost_estimate=pl.CostEstimate(
                flops=share * 2 * TILE * TILE * width,
                transcendentals=share * TILE * TILE,
                bytes_accessed=share * 2 * TILE * width * 2,
            ),
            compiler_params=params(),
            name="build",
        )(pairs, bounds, place, table_a, a_other, *group, store, kv)

    kv = jnp.zeros((NC * ABLK, TILE), F32)
    store, kv = build(0, (table_b,), store, kv)
    first_two = go(right, True, -1)
    left_down, right_down = go(left, False, 1), go(right, False, 1)
    left_up, right_up = go(left, False, -1), go(right, False, -1)
    store, kv = build(1, (left, right, down, up), store, kv)
    first_two, down, kv = lax.optimization_barrier((first_two, down, kv))
    two_up, two_down, second_two = go(first_two, False, -1), go(first_two, False, 1), go(down, False, 1)
    left_two, right_two = go(left_up, False, -1), go(right_down, False, 1)
    store, kv = build(5, (first_two, left_down, right_down, left_up, right_up), store, kv)
    two_up, kv = lax.optimization_barrier((two_up, kv))
    both_two = go(two_up, False, -1)
    store, kv = build(10, (second_two, two_down, two_up, left_two, right_two), store, kv)
    store, kv = build(15, (both_two,), store, kv)

    def half(over_rows, parts, copies, store):
        last = copies == 0
        sums = jax.ShapeDtypeStruct((NCHIP, TILE // LANES, LANES) if last else (copies, NCHIP, TILE), F32)
        logs = jax.ShapeDtypeStruct((ABLK * TILE // LANES, LANES), F32)
        return pl.pallas_call(
            lambda *refs: pass_kernel(over_rows, last, *refs),
            out_shape=(sums, logs if last else pltpu.VMEM((CAP, TILE, TILE), BF16)),
            in_specs=[SM, SM, SM, VM, VM],
            out_specs=(VM, VM),
            scratch_shapes=[pltpu.VMEM((NCHIP, TILE), F32), pltpu.VMEM((NCHIP, TILE), F32)],
            input_output_aliases={} if last else {4: 1},
            compiler_params=params(),
            name="rows" if over_rows else "columns",
        )(pairs, bounds, place, parts, store)

    for step in range(ITERS):
        if step:
            kv, store = half(True, ktu_parts, NC * NZ, store)
        kv_parts = lax.all_to_all(kv, ("core", "z"), 0, 0, tiled=True)
        if step < ITERS - 1:
            ktu, store = half(False, kv_parts, NCHIP, store)
            ktu_parts = lax.all_to_all(ktu, ("y", "x"), 0, 0, tiled=True)
    ktu, log_u = half(False, kv_parts, 0, store)
    mine = lax.all_to_all(ktu, ("y", "x"), 0, 0, tiled=True)
    log_v = jnp.log(1.0 / (1.0 + jnp.sum(mine, axis=0)))
    return log_u.reshape(-1), log_v.reshape(-1)


def solution(mesh):
    fine = jax.sharding.Mesh(mesh.devices.reshape(NY, NX, NC, NZ), ("y", "x", "core", "z"))
    a_axes = ("y", "x", "core")
    b_axes = ("z", "y", "x", "core")
    in_specs = (P(a_axes, None), P(b_axes, None), P(a_axes, "z", None), P(a_axes, "z", None), P(a_axes, "z"))
    out_specs = (P(a_axes), P(b_axes))
    return jax.shard_map(on_device, mesh=fine, in_specs=in_specs, out_specs=out_specs, check_vma=False)
```

```python
import math

import jax
import jax.numpy as jnp
from jax import lax
from jax.experimental import pallas as pl
from jax.experimental.pallas import tpu as pltpu
from jax.sharding import PartitionSpec as P

TILE = 512
ABLK = 8
ITERS = 3
LANES = 128
BUILD_STEP = 2
BUFFERS = 4
ROW_STEP = 4
COLUMN_STEP = 8
NY, NX, NC, NZ = 4, 4, 2, 4
NCHIP = NY * NX
SLOTS = 32
CAP = NC * SLOTS
F32 = jnp.float32
BF16 = jnp.bfloat16
VM = pl.BlockSpec(memory_space=pltpu.VMEM)
SM = pl.BlockSpec(memory_space=pltpu.SMEM)
ANY = pl.BlockSpec(memory_space=pl.ANY)
HB = pl.BlockSpec(memory_space=pltpu.HBM)


ORDER = (
    ((0, 0),),
    ((3, 0), (1, 0), (0, 3), (0, 1)),
    ((2, 0), (3, 3), (1, 3), (3, 1), (1, 1)),
    ((0, 2), (2, 3), (2, 1), (3, 2), (1, 2)),
    ((2, 2),),
)


def plan_kernel(lists, place, table, pairs, bounds, tally):
    core, my_y, my_x = place[0], place[1], place[2]
    for k in range(NCHIP + 1):
        tally[k] = 0

    def scan(body):
        for which in range(NC):
            live = lists[which, 2 * SLOTS]

            def step(s, carry, which=which):
                b = lists[which, SLOTS + s]

                @pl.when((b % NC) == core)
                def _():
                    chip = b // NC
                    dy = (chip // NX - my_y + NY) % NY
                    dx = (chip % NX - my_x + NX) % NX
                    code = jnp.where(core == 0, dx * NY + dy, dy * NX + dx)
                    body(which * ABLK + lists[which, s], chip, table[code])

                return carry

            lax.fori_loop(0, jnp.minimum(live, SLOTS), step, 0)

    def count(a, chip, rank):
        tally[rank + 1] = tally[rank + 1] + 1

    scan(count)
    for k in range(NCHIP):
        tally[k + 1] = tally[k + 1] + tally[k]
    for k in range(NCHIP + 1):
        bounds[k] = tally[k]

    def put(a, chip, rank):
        spot = tally[rank]
        pairs[0, spot] = a
        pairs[1, spot] = chip
        pairs[2, spot] = rank
        tally[rank] = spot + 1

    scan(put)


def room_kernel(pairs, bounds, place, store):
    pass


def build_kernel(scale, first, blocks, last, pairs, bounds, place, a_mine, a_other, *refs):
    b_refs, (_, kv_in, store, out), scratch = refs[:blocks], refs[blocks : blocks + 4], refs[blocks + 4 :]
    kv, abuf, bbuf, a_sems, b_sems = scratch
    core = place[0]
    low, high = bounds[first], bounds[first + blocks]
    ahead = BUFFERS - BUILD_STEP

    def fetch(t):
        @pl.when(t < high)
        def _():
            a = pairs[0, t]
            slot = (t - low) % BUFFERS
            row = pl.multiple_of((a % ABLK) * TILE, TILE)

            @pl.when(a // ABLK == core)
            def _():
                pltpu.make_async_copy(a_mine.at[pl.ds(row, TILE)], abuf.at[slot], a_sems.at[slot]).start()

            @pl.when(a // ABLK != core)
            def _():
                pltpu.make_async_copy(a_other.at[pl.ds(row, TILE)], abuf.at[slot], a_sems.at[slot]).start()

    loads = [pltpu.make_async_copy(b_refs[k], bbuf.at[k], b_sems.at[k]) for k in range(blocks)]
    for load in loads:
        load.start()
    for k in range(ahead):
        fetch(low + k)
    kv[...] = kv_in[...]
    ones = jnp.ones((16, TILE), BF16)
    for load in loads:
        load.wait()

    def step(c, carry):
        base = low + c * BUILD_STEP
        for k in range(BUILD_STEP):
            fetch(base + ahead + k)
        for k in range(BUILD_STEP):

            @pl.when(base + k < high)
            def _(k=k):
                slot = (base + k - low) % BUFFERS
                pltpu.make_async_copy(a_mine.at[pl.ds(0, TILE)], abuf.at[slot], a_sems.at[slot]).wait()

        sums = []
        for k in range(BUILD_STEP):
            t = jnp.minimum(base + k, high - 1)
            block_a, block_b = abuf[(t - low) % BUFFERS], bbuf[pairs[2, t] - first]
            score = lax.dot_general(block_a, block_b, (((1,), (1,)), ((), ())), preferred_element_type=F32)
            tile = jnp.exp(score * scale).astype(BF16)
            store[t] = tile
            part = lax.dot_general(ones, tile, (((1,), (1,)), ((), ())), preferred_element_type=F32)
            sums.append((pairs[0, t], jnp.where(base + k < high, part[0:1], 0.0)))
        for a, part in sums:
            kv[pl.ds(a, 1), :] += part
        return carry

    lax.fori_loop(0, (high - low + BUILD_STEP - 1) // BUILD_STEP, step, 0)
    if last:
        spread(out, kv[...])
    else:
        out[...] = kv[...]


def spread(out, value):
    for k in range(out.shape[0]):
        out[k] = value


def pass_kernel(over_rows, last, pairs, bounds, place, parts, store, out, *refs):
    sums, weight = refs[-2:]
    scaling = 1.0 / (1.0 + jnp.sum(parts[...], axis=0))
    weight[...] = scaling.astype(BF16).astype(F32)
    if last:
        logs = jnp.log(jnp.where(place[0] == 0, scaling[:ABLK], scaling[ABLK:]))
        for k in range(ABLK):
            for q in range(TILE // LANES):
                refs[0][pl.ds(k * (TILE // LANES) + q, 1), :] = logs[k : k + 1, q * LANES : (q + 1) * LANES]
    sums[...] = jnp.zeros_like(sums)
    number = bounds[NCHIP]
    size = ROW_STEP if over_rows else COLUMN_STEP
    dims = (((1,), (1,)), ((), ())) if over_rows else (((1,), (0,)), ((), ()))

    def step(c, carry):
        found = []
        for k in range(size):
            t = c * size + k
            safe = jnp.minimum(t, number - 1)
            a = pairs[0, safe]
            b = pairs[1, safe]
            source, target = (b, a) if over_rows else (a, b)
            row = jnp.where(t < number, weight[pl.ds(source, 1), :], 0.0)
            row = jnp.broadcast_to(row, (16, TILE)).astype(BF16)
            found.append((target, lax.dot_general(row, store[safe], dims, preferred_element_type=F32)))
        for target, part in found:
            sums[pl.ds(target, 1), :] += part[0:1]
        return carry

    lax.fori_loop(0, (number + size - 1) // size, step, 0)
    if last:
        for q in range(TILE // LANES):
            out[:, q, :] = sums[:, q * LANES : (q + 1) * LANES]
    else:
        spread(out, sums[...])


def params(mib=16):
    return pltpu.CompilerParams(vmem_limit_bytes=mib << 20)


def moves(first, shift):
    pairs = []
    for y in range(NY):
        for x in range(NX):
            for c in range(NC):
                dy, dx = (0, shift) if (c == 0) == first else (shift, 0)
                there = ((y + dy) % NY * NX + (x + dx) % NX) * NC + c
                pairs.append(((y * NX + x) * NC + c, there))
    return pairs


def go(block, first, shift):
    return lax.ppermute(block, ("y", "x", "core"), moves(first, shift))


def on_device(table_a, table_b, pair_a, pair_b, pair_count):
    width = table_a.shape[1]
    scale = 2.5 / math.sqrt(width)
    core = lax.axis_index("core")
    swap = [(0, 1), (1, 0)]
    own = jnp.concatenate(
        [pair_a.reshape(1, -1), pair_b.reshape(1, -1), pair_count.reshape(1, 1), jnp.zeros((1, 63), jnp.int32)], axis=1
    )
    a_other = lax.ppermute(table_a, "core", swap)
    other = lax.ppermute(own, "core", swap)
    lists = jnp.where(core == 0, jnp.concatenate([own, other]), jnp.concatenate([other, own]))
    place = jnp.stack([core, lax.axis_index("y"), lax.axis_index("x")]).astype(jnp.int32)
    table = [0] * NCHIP
    for rank, (f, s) in enumerate(sum(ORDER, ())):
        table[f * NY + s] = rank
    left, right = go(table_b, True, 1), go(table_b, True, -1)
    down, up = go(table_b, False, 1), go(table_b, False, -1)

    pairs, bounds = pl.pallas_call(
        plan_kernel,
        out_shape=(jax.ShapeDtypeStruct((3, CAP), jnp.int32), jax.ShapeDtypeStruct((NCHIP + 1,), jnp.int32)),
        in_specs=[SM, SM, SM],
        out_specs=(SM, SM),
        scratch_shapes=[pltpu.SMEM((NCHIP + 1,), jnp.int32)],
        compiler_params=params(1),
        name="plan",
    )(lists, place, jnp.array(table, jnp.int32))

    store = pl.pallas_call(
        room_kernel,
        out_shape=pltpu.VMEM((CAP, TILE, TILE), BF16),
        in_specs=[SM, SM, SM],
        out_specs=VM,
        compiler_params=params(),
        name="room",
    )(pairs, bounds, place)

    def build(first, group, store, kv):
        blocks = len(group)
        last = first + blocks == NCHIP
        shape = (NC * NZ, NC * ABLK, TILE) if last else (NC * ABLK, TILE)
        share = 2 * blocks
        return pl.pallas_call(
            lambda *refs: build_kernel(scale, first, blocks, last, *refs),
            out_shape=(pltpu.VMEM((CAP, TILE, TILE), BF16), jax.ShapeDtypeStruct(shape, F32)),
            in_specs=[SM, SM, SM, HB, HB] + [ANY] * blocks + [VM, VM],
            out_specs=(VM, VM),
            scratch_shapes=[
                pltpu.VMEM((NC * ABLK, TILE), F32),
                pltpu.VMEM((BUFFERS, TILE, width), BF16),
                pltpu.VMEM((blocks, TILE, width), BF16),
                pltpu.SemaphoreType.DMA((BUFFERS,)),
                pltpu.SemaphoreType.DMA((blocks,)),
            ],
            input_output_aliases={5 + blocks: 0},
            cost_estimate=pl.CostEstimate(
                flops=share * 2 * TILE * TILE * width,
                transcendentals=share * TILE * TILE,
                bytes_accessed=share * 2 * TILE * width * 2,
            ),
            compiler_params=params(),
            name="build",
        )(pairs, bounds, place, table_a, a_other, *group, store, kv)

    kv = jnp.zeros((NC * ABLK, TILE), F32)
    store, kv = build(0, (table_b,), store, kv)
    left, right, bounds = lax.optimization_barrier((left, right, bounds))
    first_two = go(right, True, -1)
    left_down, right_down = go(left, False, 1), go(right, False, 1)
    left_up, right_up = go(left, False, -1), go(right, False, -1)
    store, kv = build(1, (left, right, down, up), store, kv)
    first_two, down, kv = lax.optimization_barrier((first_two, down, kv))
    two_up, two_down, second_two = go(first_two, False, -1), go(first_two, False, 1), go(down, False, 1)
    left_two, right_two = go(left_up, False, -1), go(right_down, False, 1)
    store, kv = build(5, (first_two, left_down, right_down, left_up, right_up), store, kv)
    two_up, kv = lax.optimization_barrier((two_up, kv))
    both_two = go(two_up, False, -1)
    store, kv = build(10, (second_two, two_down, two_up, left_two, right_two), store, kv)
    store, kv = build(15, (both_two,), store, kv)

    def half(over_rows, parts, copies, store):
        last = copies == 0
        sums = jax.ShapeDtypeStruct((NCHIP, TILE // LANES, LANES) if last else (copies, NCHIP, TILE), F32)
        logs = jax.ShapeDtypeStruct((ABLK * TILE // LANES, LANES), F32)
        return pl.pallas_call(
            lambda *refs: pass_kernel(over_rows, last, *refs),
            out_shape=(sums, logs if last else pltpu.VMEM((CAP, TILE, TILE), BF16)),
            in_specs=[SM, SM, SM, VM, VM],
            out_specs=(VM, VM),
            scratch_shapes=[pltpu.VMEM((NCHIP, TILE), F32), pltpu.VMEM((NCHIP, TILE), F32)],
            input_output_aliases={} if last else {4: 1},
            compiler_params=params(),
            name="rows" if over_rows else "columns",
        )(pairs, bounds, place, parts, store)

    for step in range(ITERS):
        if step:
            kv, store = half(True, ktu_parts, NC * NZ, store)
        kv_parts = lax.all_to_all(kv, ("core", "z"), 0, 0, tiled=True)
        if step < ITERS - 1:
            ktu, store = half(False, kv_parts, NCHIP, store)
            ktu_parts = lax.all_to_all(ktu, ("y", "x"), 0, 0, tiled=True)
    ktu, log_u = half(False, kv_parts, 0, store)
    mine = lax.all_to_all(ktu, ("y", "x"), 0, 0, tiled=True)
    log_v = jnp.log(1.0 / (1.0 + jnp.sum(mine, axis=0)))
    return log_u.reshape(-1), log_v.reshape(-1)


def solution(mesh):
    fine = jax.sharding.Mesh(mesh.devices.reshape(NY, NX, NC, NZ), ("y", "x", "core", "z"))
    a_axes = ("y", "x", "core")
    b_axes = ("z", "y", "x", "core")
    in_specs = (P(a_axes, None), P(b_axes, None), P(a_axes, "z", None), P(a_axes, "z", None), P(a_axes, "z"))
    out_specs = (P(a_axes), P(b_axes))
    return jax.shard_map(on_device, mesh=fine, in_specs=in_specs, out_specs=out_specs, check_vma=False)
```

```python
import math

import jax
import jax.numpy as jnp
from jax import lax
from jax.experimental import pallas as pl
from jax.experimental.pallas import tpu as pltpu
from jax.sharding import PartitionSpec as P

TILE = 512
ABLK = 8
ITERS = 3
LANES = 128
BUILD_STEP = 2
BUFFERS = 4
ROW_STEP = 4
COLUMN_STEP = 8
NY, NX, NC, NZ = 4, 4, 2, 4
NCHIP = NY * NX
SLOTS = 32
CAP = NC * SLOTS
F32 = jnp.float32
BF16 = jnp.bfloat16
VM = pl.BlockSpec(memory_space=pltpu.VMEM)
SM = pl.BlockSpec(memory_space=pltpu.SMEM)
ANY = pl.BlockSpec(memory_space=pl.ANY)
HB = pl.BlockSpec(memory_space=pltpu.HBM)


ORDER = (
    ((0, 0), (3, 0), (1, 0), (0, 3), (0, 1)),
    ((2, 0), (1, 3)),
    ((3, 1), (1, 1), (3, 3)),
    ((2, 1), (1, 2), (3, 2)),
    ((0, 2), (2, 3), (2, 2)),
)


def plan_kernel(lists, place, table, pairs, bounds, tally):
    core, my_y, my_x = place[0], place[1], place[2]
    for k in range(NCHIP + 1):
        tally[k] = 0

    def scan(body):
        for which in range(NC):
            live = lists[which, 2 * SLOTS]

            def step(s, carry, which=which):
                b = lists[which, SLOTS + s]

                @pl.when((b % NC) == core)
                def _():
                    chip = b // NC
                    dy = (chip // NX - my_y + NY) % NY
                    dx = (chip % NX - my_x + NX) % NX
                    code = jnp.where(core == 0, dx * NY + dy, dy * NX + dx)
                    body(which * ABLK + lists[which, s], chip, table[code])

                return carry

            lax.fori_loop(0, jnp.minimum(live, SLOTS), step, 0)

    def count(a, chip, rank):
        tally[rank + 1] = tally[rank + 1] + 1

    scan(count)
    for k in range(NCHIP):
        tally[k + 1] = tally[k + 1] + tally[k]
    for k in range(NCHIP + 1):
        bounds[k] = tally[k]

    def put(a, chip, rank):
        spot = tally[rank]
        pairs[0, spot] = a
        pairs[1, spot] = chip
        pairs[2, spot] = rank
        tally[rank] = spot + 1

    scan(put)


def room_kernel(pairs, bounds, place, store):
    pass


def build_kernel(scale, first, blocks, last, pairs, bounds, place, a_mine, a_other, *refs):
    b_refs, (_, kv_in, store, out), scratch = refs[:blocks], refs[blocks : blocks + 4], refs[blocks + 4 :]
    kv, abuf, bbuf, a_sems, b_sems = scratch
    core = place[0]
    low, high = bounds[first], bounds[first + blocks]
    ahead = BUFFERS - BUILD_STEP

    def fetch(t):
        @pl.when(t < high)
        def _():
            a = pairs[0, t]
            slot = (t - low) % BUFFERS
            row = pl.multiple_of((a % ABLK) * TILE, TILE)

            @pl.when(a // ABLK == core)
            def _():
                pltpu.make_async_copy(a_mine.at[pl.ds(row, TILE)], abuf.at[slot], a_sems.at[slot]).start()

            @pl.when(a // ABLK != core)
            def _():
                pltpu.make_async_copy(a_other.at[pl.ds(row, TILE)], abuf.at[slot], a_sems.at[slot]).start()

    loads = [pltpu.make_async_copy(b_refs[k], bbuf.at[k], b_sems.at[k]) for k in range(blocks)]
    for load in loads:
        load.start()
    for k in range(ahead):
        fetch(low + k)
    kv[...] = kv_in[...]
    ones = jnp.ones((16, TILE), BF16)
    for load in loads:
        load.wait()

    def step(c, carry):
        base = low + c * BUILD_STEP
        for k in range(BUILD_STEP):
            fetch(base + ahead + k)
        for k in range(BUILD_STEP):

            @pl.when(base + k < high)
            def _(k=k):
                slot = (base + k - low) % BUFFERS
                pltpu.make_async_copy(a_mine.at[pl.ds(0, TILE)], abuf.at[slot], a_sems.at[slot]).wait()

        sums = []
        for k in range(BUILD_STEP):
            t = jnp.minimum(base + k, high - 1)
            block_a, block_b = abuf[(t - low) % BUFFERS], bbuf[pairs[2, t] - first]
            score = lax.dot_general(block_a, block_b, (((1,), (1,)), ((), ())), preferred_element_type=F32)
            tile = jnp.exp(score * scale).astype(BF16)
            store[t] = tile
            part = lax.dot_general(ones, tile, (((1,), (1,)), ((), ())), preferred_element_type=F32)
            sums.append((pairs[0, t], jnp.where(base + k < high, part[0:1], 0.0)))
        for a, part in sums:
            kv[pl.ds(a, 1), :] += part
        return carry

    lax.fori_loop(0, (high - low + BUILD_STEP - 1) // BUILD_STEP, step, 0)
    if last:
        spread(out, kv[...])
    else:
        out[...] = kv[...]


def spread(out, value):
    for k in range(out.shape[0]):
        out[k] = value


def pass_kernel(over_rows, last, pairs, bounds, place, parts, store, out, *refs):
    sums, weight = refs[-2:]
    scaling = 1.0 / (1.0 + jnp.sum(parts[...], axis=0))
    weight[...] = scaling.astype(BF16).astype(F32)
    if last:
        logs = jnp.log(jnp.where(place[0] == 0, scaling[:ABLK], scaling[ABLK:]))
        for k in range(ABLK):
            for q in range(TILE // LANES):
                refs[0][pl.ds(k * (TILE // LANES) + q, 1), :] = logs[k : k + 1, q * LANES : (q + 1) * LANES]
    sums[...] = jnp.zeros_like(sums)
    number = bounds[NCHIP]
    size = ROW_STEP if over_rows else COLUMN_STEP
    dims = (((1,), (1,)), ((), ())) if over_rows else (((1,), (0,)), ((), ()))

    def step(c, carry):
        found = []
        for k in range(size):
            t = c * size + k
            safe = jnp.minimum(t, number - 1)
            a = pairs[0, safe]
            b = pairs[1, safe]
            source, target = (b, a) if over_rows else (a, b)
            row = jnp.where(t < number, weight[pl.ds(source, 1), :], 0.0)
            row = jnp.broadcast_to(row, (16, TILE)).astype(BF16)
            found.append((target, lax.dot_general(row, store[safe], dims, preferred_element_type=F32)))
        for target, part in found:
            sums[pl.ds(target, 1), :] += part[0:1]
        return carry

    lax.fori_loop(0, (number + size - 1) // size, step, 0)
    if last:
        for q in range(TILE // LANES):
            out[:, q, :] = sums[:, q * LANES : (q + 1) * LANES]
    else:
        spread(out, sums[...])


def params(mib=16):
    return pltpu.CompilerParams(vmem_limit_bytes=mib << 20)


def moves(first, shift):
    pairs = []
    for y in range(NY):
        for x in range(NX):
            for c in range(NC):
                dy, dx = (0, shift) if (c == 0) == first else (shift, 0)
                there = ((y + dy) % NY * NX + (x + dx) % NX) * NC + c
                pairs.append(((y * NX + x) * NC + c, there))
    return pairs


def go(block, first, shift):
    return lax.ppermute(block, ("y", "x", "core"), moves(first, shift))


def on_device(table_a, table_b, pair_a, pair_b, pair_count):
    width = table_a.shape[1]
    scale = 2.5 / math.sqrt(width)
    core = lax.axis_index("core")
    swap = [(0, 1), (1, 0)]
    own = jnp.concatenate(
        [pair_a.reshape(1, -1), pair_b.reshape(1, -1), pair_count.reshape(1, 1), jnp.zeros((1, 63), jnp.int32)], axis=1
    )
    a_other = lax.ppermute(table_a, "core", swap)
    other = lax.ppermute(own, "core", swap)
    lists = jnp.where(core == 0, jnp.concatenate([own, other]), jnp.concatenate([other, own]))
    place = jnp.stack([core, lax.axis_index("y"), lax.axis_index("x")]).astype(jnp.int32)
    table = [0] * NCHIP
    for rank, (f, s) in enumerate(sum(ORDER, ())):
        table[f * NY + s] = rank
    left, right = go(table_b, True, 1), go(table_b, True, -1)
    down, up = go(table_b, False, 1), go(table_b, False, -1)

    pairs, bounds = pl.pallas_call(
        plan_kernel,
        out_shape=(jax.ShapeDtypeStruct((3, CAP), jnp.int32), jax.ShapeDtypeStruct((NCHIP + 1,), jnp.int32)),
        in_specs=[SM, SM, SM],
        out_specs=(SM, SM),
        scratch_shapes=[pltpu.SMEM((NCHIP + 1,), jnp.int32)],
        compiler_params=params(1),
        name="plan",
    )(lists, place, jnp.array(table, jnp.int32))

    store = pl.pallas_call(
        room_kernel,
        out_shape=pltpu.VMEM((CAP, TILE, TILE), BF16),
        in_specs=[SM, SM, SM],
        out_specs=VM,
        compiler_params=params(),
        name="room",
    )(pairs, bounds, place)

    def build(first, group, store, kv):
        blocks = len(group)
        last = first + blocks == NCHIP
        shape = (NC * NZ, NC * ABLK, TILE) if last else (NC * ABLK, TILE)
        share = 2 * blocks
        return pl.pallas_call(
            lambda *refs: build_kernel(scale, first, blocks, last, *refs),
            out_shape=(pltpu.VMEM((CAP, TILE, TILE), BF16), jax.ShapeDtypeStruct(shape, F32)),
            in_specs=[SM, SM, SM, HB, HB] + [ANY] * blocks + [VM, VM],
            out_specs=(VM, VM),
            scratch_shapes=[
                pltpu.VMEM((NC * ABLK, TILE), F32),
                pltpu.VMEM((BUFFERS, TILE, width), BF16),
                pltpu.VMEM((blocks, TILE, width), BF16),
                pltpu.SemaphoreType.DMA((BUFFERS,)),
                pltpu.SemaphoreType.DMA((blocks,)),
            ],
            input_output_aliases={5 + blocks: 0},
            cost_estimate=pl.CostEstimate(
                flops=share * 2 * TILE * TILE * width,
                transcendentals=share * TILE * TILE,
                bytes_accessed=share * 2 * TILE * width * 2,
            ),
            compiler_params=params(),
            name="build",
        )(pairs, bounds, place, table_a, a_other, *group, store, kv)

    kv = jnp.zeros((NC * ABLK, TILE), F32)
    left, right, bounds = lax.optimization_barrier((left, right, bounds))
    first_two = go(right, True, -1)
    left_down, right_down = go(left, False, 1), go(right, False, 1)
    left_up, right_up = go(left, False, -1), go(right, False, -1)
    store, kv = build(0, (table_b, left, right, down, up), store, kv)
    first_two, right_down, down, kv = lax.optimization_barrier((first_two, right_down, down, kv))
    two_up, two_down, second_two = go(first_two, False, -1), go(first_two, False, 1), go(down, False, 1)
    right_two = go(right_down, False, 1)
    store, kv = build(5, (first_two, right_down), store, kv)
    left_up, right_up, left_down, kv = lax.optimization_barrier((left_up, right_up, left_down, kv))
    left_two = go(left_up, False, -1)
    store, kv = build(7, (left_up, right_up, left_down), store, kv)
    two_up, kv = lax.optimization_barrier((two_up, kv))
    both_two = go(two_up, False, -1)
    store, kv = build(10, (two_up, right_two, left_two), store, kv)
    second_two, two_down, both_two, kv = lax.optimization_barrier((second_two, two_down, both_two, kv))
    store, kv = build(13, (second_two, two_down, both_two), store, kv)

    def half(over_rows, parts, copies, store):
        last = copies == 0
        sums = jax.ShapeDtypeStruct((NCHIP, TILE // LANES, LANES) if last else (copies, NCHIP, TILE), F32)
        logs = jax.ShapeDtypeStruct((ABLK * TILE // LANES, LANES), F32)
        return pl.pallas_call(
            lambda *refs: pass_kernel(over_rows, last, *refs),
            out_shape=(sums, logs if last else pltpu.VMEM((CAP, TILE, TILE), BF16)),
            in_specs=[SM, SM, SM, VM, VM],
            out_specs=(VM, VM),
            scratch_shapes=[pltpu.VMEM((NCHIP, TILE), F32), pltpu.VMEM((NCHIP, TILE), F32)],
            input_output_aliases={} if last else {4: 1},
            compiler_params=params(),
            name="rows" if over_rows else "columns",
        )(pairs, bounds, place, parts, store)

    for step in range(ITERS):
        if step:
            kv, store = half(True, ktu_parts, NC * NZ, store)
        kv_parts = lax.all_to_all(kv, ("core", "z"), 0, 0, tiled=True)
        if step < ITERS - 1:
            ktu, store = half(False, kv_parts, NCHIP, store)
            ktu_parts = lax.all_to_all(ktu, ("y", "x"), 0, 0, tiled=True)
    ktu, log_u = half(False, kv_parts, 0, store)
    mine = lax.all_to_all(ktu, ("y", "x"), 0, 0, tiled=True)
    log_v = jnp.log(1.0 / (1.0 + jnp.sum(mine, axis=0)))
    return log_u.reshape(-1), log_v.reshape(-1)


def solution(mesh):
    fine = jax.sharding.Mesh(mesh.devices.reshape(NY, NX, NC, NZ), ("y", "x", "core", "z"))
    a_axes = ("y", "x", "core")
    b_axes = ("z", "y", "x", "core")
    in_specs = (P(a_axes, None), P(b_axes, None), P(a_axes, "z", None), P(a_axes, "z", None), P(a_axes, "z"))
    out_specs = (P(a_axes), P(b_axes))
    return jax.shard_map(on_device, mesh=fine, in_specs=in_specs, out_specs=out_specs, check_vma=False)
```

```python
import math

import jax
import jax.numpy as jnp
from jax import lax
from jax.experimental import pallas as pl
from jax.experimental.pallas import tpu as pltpu
from jax.sharding import PartitionSpec as P

TILE = 512
ABLK = 8
ITERS = 3
LANES = 128
BUILD_STEP = 2
BUFFERS = 4
ROW_STEP = 4
COLUMN_STEP = 8
NY, NX, NC, NZ = 4, 4, 2, 4
NCHIP = NY * NX
SLOTS = 32
CAP = NC * SLOTS
F32 = jnp.float32
BF16 = jnp.bfloat16
VM = pl.BlockSpec(memory_space=pltpu.VMEM)
SM = pl.BlockSpec(memory_space=pltpu.SMEM)
ANY = pl.BlockSpec(memory_space=pl.ANY)
HB = pl.BlockSpec(memory_space=pltpu.HBM)


ORDER = (
    ((0, 0), (3, 0), (1, 0), (0, 3), (0, 1)),
    ((2, 0), (1, 3)),
    ((3, 1), (1, 1), (3, 3)),
    ((2, 1), (1, 2)),
    ((3, 2), (0, 2), (2, 3)),
    ((2, 2),),
)


def plan_kernel(lists, place, table, pairs, bounds, tally):
    core, my_y, my_x = place[0], place[1], place[2]
    for k in range(NCHIP + 1):
        tally[k] = 0

    def scan(body):
        for which in range(NC):
            live = lists[which, 2 * SLOTS]

            def step(s, carry, which=which):
                b = lists[which, SLOTS + s]

                @pl.when((b % NC) == core)
                def _():
                    chip = b // NC
                    dy = (chip // NX - my_y + NY) % NY
                    dx = (chip % NX - my_x + NX) % NX
                    code = jnp.where(core == 0, dx * NY + dy, dy * NX + dx)
                    body(which * ABLK + lists[which, s], chip, table[code])

                return carry

            lax.fori_loop(0, jnp.minimum(live, SLOTS), step, 0)

    def count(a, chip, rank):
        tally[rank + 1] = tally[rank + 1] + 1

    scan(count)
    for k in range(NCHIP):
        tally[k + 1] = tally[k + 1] + tally[k]
    for k in range(NCHIP + 1):
        bounds[k] = tally[k]

    def put(a, chip, rank):
        spot = tally[rank]
        pairs[0, spot] = a
        pairs[1, spot] = chip
        pairs[2, spot] = rank
        tally[rank] = spot + 1

    scan(put)


def room_kernel(pairs, bounds, place, store):
    pass


def build_kernel(scale, first, blocks, last, pairs, bounds, place, a_mine, a_other, *refs):
    b_refs, (_, kv_in, store, out), scratch = refs[:blocks], refs[blocks : blocks + 4], refs[blocks + 4 :]
    kv, abuf, bbuf, a_sems, b_sems = scratch
    core = place[0]
    low, high = bounds[first], bounds[first + blocks]
    ahead = BUFFERS - BUILD_STEP

    def fetch(t):
        @pl.when(t < high)
        def _():
            a = pairs[0, t]
            slot = (t - low) % BUFFERS
            row = pl.multiple_of((a % ABLK) * TILE, TILE)

            @pl.when(a // ABLK == core)
            def _():
                pltpu.make_async_copy(a_mine.at[pl.ds(row, TILE)], abuf.at[slot], a_sems.at[slot]).start()

            @pl.when(a // ABLK != core)
            def _():
                pltpu.make_async_copy(a_other.at[pl.ds(row, TILE)], abuf.at[slot], a_sems.at[slot]).start()

    loads = [pltpu.make_async_copy(b_refs[k], bbuf.at[k], b_sems.at[k]) for k in range(blocks)]
    for load in loads:
        load.start()
    for k in range(ahead):
        fetch(low + k)
    kv[...] = kv_in[...]
    ones = jnp.ones((16, TILE), BF16)
    for load in loads:
        load.wait()

    def step(c, carry):
        base = low + c * BUILD_STEP
        for k in range(BUILD_STEP):
            fetch(base + ahead + k)
        for k in range(BUILD_STEP):

            @pl.when(base + k < high)
            def _(k=k):
                slot = (base + k - low) % BUFFERS
                pltpu.make_async_copy(a_mine.at[pl.ds(0, TILE)], abuf.at[slot], a_sems.at[slot]).wait()

        sums = []
        for k in range(BUILD_STEP):
            t = jnp.minimum(base + k, high - 1)
            block_a, block_b = abuf[(t - low) % BUFFERS], bbuf[pairs[2, t] - first]
            score = lax.dot_general(block_a, block_b, (((1,), (1,)), ((), ())), preferred_element_type=F32)
            tile = jnp.exp(score * scale).astype(BF16)
            store[t] = tile
            part = lax.dot_general(ones, tile, (((1,), (1,)), ((), ())), preferred_element_type=F32)
            sums.append((pairs[0, t], jnp.where(base + k < high, part[0:1], 0.0)))
        for a, part in sums:
            kv[pl.ds(a, 1), :] += part
        return carry

    lax.fori_loop(0, (high - low + BUILD_STEP - 1) // BUILD_STEP, step, 0)
    if last:
        spread(out, kv[...])
    else:
        out[...] = kv[...]


def spread(out, value):
    for k in range(out.shape[0]):
        out[k] = value


def pass_kernel(over_rows, last, pairs, bounds, place, parts, store, out, *refs):
    sums, weight = refs[-2:]
    scaling = 1.0 / (1.0 + jnp.sum(parts[...], axis=0))
    weight[...] = scaling.astype(BF16).astype(F32)
    if last:
        logs = jnp.log(jnp.where(place[0] == 0, scaling[:ABLK], scaling[ABLK:]))
        for k in range(ABLK):
            for q in range(TILE // LANES):
                refs[0][pl.ds(k * (TILE // LANES) + q, 1), :] = logs[k : k + 1, q * LANES : (q + 1) * LANES]
    sums[...] = jnp.zeros_like(sums)
    number = bounds[NCHIP]
    size = ROW_STEP if over_rows else COLUMN_STEP
    dims = (((1,), (1,)), ((), ())) if over_rows else (((1,), (0,)), ((), ()))

    def step(c, carry):
        found = []
        for k in range(size):
            t = c * size + k
            safe = jnp.minimum(t, number - 1)
            a = pairs[0, safe]
            b = pairs[1, safe]
            source, target = (b, a) if over_rows else (a, b)
            row = jnp.where(t < number, weight[pl.ds(source, 1), :], 0.0)
            row = jnp.broadcast_to(row, (16, TILE)).astype(BF16)
            found.append((target, lax.dot_general(row, store[safe], dims, preferred_element_type=F32)))
        for target, part in found:
            sums[pl.ds(target, 1), :] += part[0:1]
        return carry

    lax.fori_loop(0, (number + size - 1) // size, step, 0)
    if last:
        for q in range(TILE // LANES):
            out[:, q, :] = sums[:, q * LANES : (q + 1) * LANES]
    else:
        spread(out, sums[...])


def params(mib=16):
    return pltpu.CompilerParams(vmem_limit_bytes=mib << 20)


def moves(first, shift):
    pairs = []
    for y in range(NY):
        for x in range(NX):
            for c in range(NC):
                dy, dx = (0, shift) if (c == 0) == first else (shift, 0)
                there = ((y + dy) % NY * NX + (x + dx) % NX) * NC + c
                pairs.append(((y * NX + x) * NC + c, there))
    return pairs


def go(block, first, shift):
    return lax.ppermute(block, ("y", "x", "core"), moves(first, shift))


def on_device(table_a, table_b, pair_a, pair_b, pair_count):
    width = table_a.shape[1]
    scale = 2.5 / math.sqrt(width)
    core = lax.axis_index("core")
    swap = [(0, 1), (1, 0)]
    own = jnp.concatenate(
        [pair_a.reshape(1, -1), pair_b.reshape(1, -1), pair_count.reshape(1, 1), jnp.zeros((1, 63), jnp.int32)], axis=1
    )
    a_other = lax.ppermute(table_a, "core", swap)
    other = lax.ppermute(own, "core", swap)
    lists = jnp.where(core == 0, jnp.concatenate([own, other]), jnp.concatenate([other, own]))
    place = jnp.stack([core, lax.axis_index("y"), lax.axis_index("x")]).astype(jnp.int32)
    table = [0] * NCHIP
    for rank, (f, s) in enumerate(sum(ORDER, ())):
        table[f * NY + s] = rank
    left, right = go(table_b, True, 1), go(table_b, True, -1)
    down, up = go(table_b, False, 1), go(table_b, False, -1)

    pairs, bounds = pl.pallas_call(
        plan_kernel,
        out_shape=(jax.ShapeDtypeStruct((3, CAP), jnp.int32), jax.ShapeDtypeStruct((NCHIP + 1,), jnp.int32)),
        in_specs=[SM, SM, SM],
        out_specs=(SM, SM),
        scratch_shapes=[pltpu.SMEM((NCHIP + 1,), jnp.int32)],
        compiler_params=params(1),
        name="plan",
    )(lists, place, jnp.array(table, jnp.int32))

    store = pl.pallas_call(
        room_kernel,
        out_shape=pltpu.VMEM((CAP, TILE, TILE), BF16),
        in_specs=[SM, SM, SM],
        out_specs=VM,
        compiler_params=params(),
        name="room",
    )(pairs, bounds, place)

    def build(first, group, store, kv):
        blocks = len(group)
        last = first + blocks == NCHIP
        shape = (NC * NZ, NC * ABLK, TILE) if last else (NC * ABLK, TILE)
        share = 2 * blocks
        return pl.pallas_call(
            lambda *refs: build_kernel(scale, first, blocks, last, *refs),
            out_shape=(pltpu.VMEM((CAP, TILE, TILE), BF16), jax.ShapeDtypeStruct(shape, F32)),
            in_specs=[SM, SM, SM, HB, HB] + [ANY] * blocks + [VM, VM],
            out_specs=(VM, VM),
            scratch_shapes=[
                pltpu.VMEM((NC * ABLK, TILE), F32),
                pltpu.VMEM((BUFFERS, TILE, width), BF16),
                pltpu.VMEM((blocks, TILE, width), BF16),
                pltpu.SemaphoreType.DMA((BUFFERS,)),
                pltpu.SemaphoreType.DMA((blocks,)),
            ],
            input_output_aliases={5 + blocks: 0},
            cost_estimate=pl.CostEstimate(
                flops=share * 2 * TILE * TILE * width,
                transcendentals=share * TILE * TILE,
                bytes_accessed=share * 2 * TILE * width * 2,
            ),
            compiler_params=params(),
            name="build",
        )(pairs, bounds, place, table_a, a_other, *group, store, kv)

    kv = jnp.zeros((NC * ABLK, TILE), F32)
    left, right, bounds = lax.optimization_barrier((left, right, bounds))
    first_two = go(right, True, -1)
    left_down, right_down = go(left, False, 1), go(right, False, 1)
    left_up, right_up = go(left, False, -1), go(right, False, -1)
    store, kv = build(0, (table_b, left, right, down, up), store, kv)
    first_two, right_down, down, kv = lax.optimization_barrier((first_two, right_down, down, kv))
    two_up, two_down, second_two = go(first_two, False, -1), go(first_two, False, 1), go(down, False, 1)
    right_two = go(right_down, False, 1)
    store, kv = build(5, (first_two, right_down), store, kv)
    left_up, right_up, left_down, kv = lax.optimization_barrier((left_up, right_up, left_down, kv))
    left_two = go(left_up, False, -1)
    store, kv = build(7, (left_up, right_up, left_down), store, kv)
    two_up, kv = lax.optimization_barrier((two_up, kv))
    both_two = go(two_up, False, -1)
    store, kv = build(10, (two_up, right_two), store, kv)
    left_two, second_two, two_down, kv = lax.optimization_barrier((left_two, second_two, two_down, kv))
    store, kv = build(12, (left_two, second_two, two_down), store, kv)
    both_two, kv = lax.optimization_barrier((both_two, kv))
    store, kv = build(15, (both_two,), store, kv)

    def half(over_rows, parts, copies, store):
        last = copies == 0
        sums = jax.ShapeDtypeStruct((NCHIP, TILE // LANES, LANES) if last else (copies, NCHIP, TILE), F32)
        logs = jax.ShapeDtypeStruct((ABLK * TILE // LANES, LANES), F32)
        return pl.pallas_call(
            lambda *refs: pass_kernel(over_rows, last, *refs),
            out_shape=(sums, logs if last else pltpu.VMEM((CAP, TILE, TILE), BF16)),
            in_specs=[SM, SM, SM, VM, VM],
            out_specs=(VM, VM),
            scratch_shapes=[pltpu.VMEM((NCHIP, TILE), F32), pltpu.VMEM((NCHIP, TILE), F32)],
            input_output_aliases={} if last else {4: 1},
            compiler_params=params(),
            name="rows" if over_rows else "columns",
        )(pairs, bounds, place, parts, store)

    for step in range(ITERS):
        if step:
            kv, store = half(True, ktu_parts, NC * NZ, store)
        kv_parts = lax.all_to_all(kv, ("core", "z"), 0, 0, tiled=True)
        if step < ITERS - 1:
            ktu, store = half(False, kv_parts, NCHIP, store)
            ktu_parts = lax.all_to_all(ktu, ("y", "x"), 0, 0, tiled=True)
    ktu, log_u = half(False, kv_parts, 0, store)
    mine = lax.all_to_all(ktu, ("y", "x"), 0, 0, tiled=True)
    log_v = jnp.log(1.0 / (1.0 + jnp.sum(mine, axis=0)))
    return log_u.reshape(-1), log_v.reshape(-1)


def solution(mesh):
    fine = jax.sharding.Mesh(mesh.devices.reshape(NY, NX, NC, NZ), ("y", "x", "core", "z"))
    a_axes = ("y", "x", "core")
    b_axes = ("z", "y", "x", "core")
    in_specs = (P(a_axes, None), P(b_axes, None), P(a_axes, "z", None), P(a_axes, "z", None), P(a_axes, "z"))
    out_specs = (P(a_axes), P(b_axes))
    return jax.shard_map(on_device, mesh=fine, in_specs=in_specs, out_specs=out_specs, check_vma=False)
```

```python
import math

import jax
import jax.numpy as jnp
from jax import lax
from jax.experimental import pallas as pl
from jax.experimental.pallas import tpu as pltpu
from jax.sharding import PartitionSpec as P

TILE = 512
ABLK = 8
ITERS = 3
LANES = 128
BUILD_STEP = 2
BUFFERS = 4
ROW_STEP = 4
COLUMN_STEP = 8
NY, NX, NC, NZ = 4, 4, 2, 4
NCHIP = NY * NX
SLOTS = 32
CAP = NC * SLOTS
F32 = jnp.float32
BF16 = jnp.bfloat16
VM = pl.BlockSpec(memory_space=pltpu.VMEM)
SM = pl.BlockSpec(memory_space=pltpu.SMEM)
ANY = pl.BlockSpec(memory_space=pl.ANY)
HB = pl.BlockSpec(memory_space=pltpu.HBM)


ORDER = (
    ((0, 0), (3, 0), (1, 0), (0, 3), (0, 1)),
    ((2, 0), (1, 3)),
    ((3, 1), (1, 1), (3, 3)),
    ((2, 1), (1, 2), (3, 2)),
    ((0, 2), (2, 3), (2, 2)),
)


def plan_kernel(lists, place, table, pairs, bounds, tally):
    core, my_y, my_x = place[0], place[1], place[2]
    for k in range(NCHIP + 1):
        tally[k] = 0

    def scan(body):
        for which in range(NC):
            live = lists[which, 2 * SLOTS]

            def step(s, carry, which=which):
                b = lists[which, SLOTS + s]

                @pl.when((b % NC) == core)
                def _():
                    chip = b // NC
                    dy = (chip // NX - my_y + NY) % NY
                    dx = (chip % NX - my_x + NX) % NX
                    code = jnp.where(core == 0, dx * NY + dy, dy * NX + dx)
                    body(which * ABLK + lists[which, s], chip, table[code])

                return carry

            lax.fori_loop(0, jnp.minimum(live, SLOTS), step, 0)

    def count(a, chip, rank):
        tally[rank + 1] = tally[rank + 1] + 1

    scan(count)
    for k in range(NCHIP):
        tally[k + 1] = tally[k + 1] + tally[k]
    for k in range(NCHIP + 1):
        bounds[k] = tally[k]

    def put(a, chip, rank):
        spot = tally[rank]
        pairs[0, spot] = a
        pairs[1, spot] = chip
        pairs[2, spot] = rank
        tally[rank] = spot + 1

    scan(put)


def room_kernel(pairs, bounds, place, store):
    pass


def build_kernel(scale, first, blocks, last, pairs, bounds, place, a_mine, a_other, *refs):
    b_refs, (_, kv_in, store, out), scratch = refs[:blocks], refs[blocks : blocks + 4], refs[blocks + 4 :]
    kv, abuf, bbuf, a_sems, b_sems = scratch
    core = place[0]
    low, high = bounds[first], bounds[first + blocks]
    ahead = BUFFERS - BUILD_STEP

    def fetch(t):
        @pl.when(t < high)
        def _():
            a = pairs[0, t]
            slot = (t - low) % BUFFERS
            row = pl.multiple_of((a % ABLK) * TILE, TILE)

            @pl.when(a // ABLK == core)
            def _():
                pltpu.make_async_copy(a_mine.at[pl.ds(row, TILE)], abuf.at[slot], a_sems.at[slot]).start()

            @pl.when(a // ABLK != core)
            def _():
                pltpu.make_async_copy(a_other.at[pl.ds(row, TILE)], abuf.at[slot], a_sems.at[slot]).start()

    loads = [pltpu.make_async_copy(b_refs[k], bbuf.at[k], b_sems.at[k]) for k in range(blocks)]
    for load in loads:
        load.start()
    for k in range(ahead):
        fetch(low + k)
    kv[...] = kv_in[...]
    ones = jnp.ones((16, TILE), BF16)
    for load in loads:
        load.wait()

    def step(c, carry):
        base = low + c * BUILD_STEP
        for k in range(BUILD_STEP):
            fetch(base + ahead + k)
        for k in range(BUILD_STEP):

            @pl.when(base + k < high)
            def _(k=k):
                slot = (base + k - low) % BUFFERS
                pltpu.make_async_copy(a_mine.at[pl.ds(0, TILE)], abuf.at[slot], a_sems.at[slot]).wait()

        sums = []
        for k in range(BUILD_STEP):
            t = jnp.minimum(base + k, high - 1)
            block_a, block_b = abuf[(t - low) % BUFFERS], bbuf[pairs[2, t] - first]
            score = lax.dot_general(block_a, block_b, (((1,), (1,)), ((), ())), preferred_element_type=F32)
            tile = jnp.exp(score * scale).astype(BF16)
            store[t] = tile
            part = lax.dot_general(ones, tile, (((1,), (1,)), ((), ())), preferred_element_type=F32)
            sums.append((pairs[0, t], jnp.where(base + k < high, part[0:1], 0.0)))
        for a, part in sums:
            kv[pl.ds(a, 1), :] += part
        return carry

    lax.fori_loop(0, (high - low + BUILD_STEP - 1) // BUILD_STEP, step, 0)
    if last:
        spread(out, kv[...])
    else:
        out[...] = kv[...]


def spread(out, value):
    for k in range(out.shape[0]):
        out[k] = value


def pass_kernel(over_rows, last, pairs, bounds, place, parts, store, out, *refs):
    sums, weight = refs[-2:]
    scaling = 1.0 / (1.0 + jnp.sum(parts[...], axis=0))
    weight[...] = scaling.astype(BF16).astype(F32)
    if last:
        logs = jnp.log(jnp.where(place[0] == 0, scaling[:ABLK], scaling[ABLK:]))
        for k in range(ABLK):
            for q in range(TILE // LANES):
                refs[0][pl.ds(k * (TILE // LANES) + q, 1), :] = logs[k : k + 1, q * LANES : (q + 1) * LANES]
    sums[...] = jnp.zeros_like(sums)
    number = bounds[NCHIP]
    size = ROW_STEP if over_rows else COLUMN_STEP
    dims = (((1,), (1,)), ((), ())) if over_rows else (((1,), (0,)), ((), ()))

    def step(c, carry):
        found = []
        for k in range(size):
            t = c * size + k
            safe = jnp.minimum(t, number - 1)
            a = pairs[0, safe]
            b = pairs[1, safe]
            source, target = (b, a) if over_rows else (a, b)
            row = jnp.where(t < number, weight[pl.ds(source, 1), :], 0.0)
            row = jnp.broadcast_to(row, (16, TILE)).astype(BF16)
            found.append((target, lax.dot_general(row, store[safe], dims, preferred_element_type=F32)))
        for target, part in found:
            sums[pl.ds(target, 1), :] += part[0:1]
        return carry

    lax.fori_loop(0, (number + size - 1) // size, step, 0)
    if last:
        for q in range(TILE // LANES):
            out[:, q, :] = sums[:, q * LANES : (q + 1) * LANES]
    else:
        spread(out, sums[...])


def params(mib=16):
    return pltpu.CompilerParams(vmem_limit_bytes=mib << 20)


def moves(first, shift):
    pairs = []
    for y in range(NY):
        for x in range(NX):
            for c in range(NC):
                dy, dx = (0, shift) if (c == 0) == first else (shift, 0)
                there = ((y + dy) % NY * NX + (x + dx) % NX) * NC + c
                pairs.append(((y * NX + x) * NC + c, there))
    return pairs


def go(block, first, shift):
    return lax.ppermute(block, ("y", "x", "core"), moves(first, shift))


def on_device(table_a, table_b, pair_a, pair_b, pair_count):
    width = table_a.shape[1]
    scale = 2.5 / math.sqrt(width)
    core = lax.axis_index("core")
    swap = [(0, 1), (1, 0)]
    own = jnp.concatenate(
        [pair_a.reshape(1, -1), pair_b.reshape(1, -1), pair_count.reshape(1, 1), jnp.zeros((1, 63), jnp.int32)], axis=1
    )
    other = lax.ppermute(own, "core", swap)
    lists = jnp.where(core == 0, jnp.concatenate([own, other]), jnp.concatenate([other, own]))
    place = jnp.stack([core, lax.axis_index("y"), lax.axis_index("x")]).astype(jnp.int32)
    table = [0] * NCHIP
    for rank, (f, s) in enumerate(sum(ORDER, ())):
        table[f * NY + s] = rank
    left, right = go(table_b, True, 1), go(table_b, True, -1)
    down, up = go(table_b, False, 1), go(table_b, False, -1)

    pairs, bounds = pl.pallas_call(
        plan_kernel,
        out_shape=(jax.ShapeDtypeStruct((3, CAP), jnp.int32), jax.ShapeDtypeStruct((NCHIP + 1,), jnp.int32)),
        in_specs=[SM, SM, SM],
        out_specs=(SM, SM),
        scratch_shapes=[pltpu.SMEM((NCHIP + 1,), jnp.int32)],
        compiler_params=params(1),
        name="plan",
    )(lists, place, jnp.array(table, jnp.int32))

    store = pl.pallas_call(
        room_kernel,
        out_shape=pltpu.VMEM((CAP, TILE, TILE), BF16),
        in_specs=[SM, SM, SM],
        out_specs=VM,
        compiler_params=params(),
        name="room",
    )(pairs, bounds, place)

    def build(first, group, store, kv):
        blocks = len(group)
        last = first + blocks == NCHIP
        shape = (NC * NZ, NC * ABLK, TILE) if last else (NC * ABLK, TILE)
        share = 2 * blocks
        return pl.pallas_call(
            lambda *refs: build_kernel(scale, first, blocks, last, *refs),
            out_shape=(pltpu.VMEM((CAP, TILE, TILE), BF16), jax.ShapeDtypeStruct(shape, F32)),
            in_specs=[SM, SM, SM, HB, HB] + [ANY] * blocks + [VM, VM],
            out_specs=(VM, VM),
            scratch_shapes=[
                pltpu.VMEM((NC * ABLK, TILE), F32),
                pltpu.VMEM((BUFFERS, TILE, width), BF16),
                pltpu.VMEM((blocks, TILE, width), BF16),
                pltpu.SemaphoreType.DMA((BUFFERS,)),
                pltpu.SemaphoreType.DMA((blocks,)),
            ],
            input_output_aliases={5 + blocks: 0},
            cost_estimate=pl.CostEstimate(
                flops=share * 2 * TILE * TILE * width,
                transcendentals=share * TILE * TILE,
                bytes_accessed=share * 2 * TILE * width * 2,
            ),
            compiler_params=params(),
            name="build",
        )(pairs, bounds, place, table_a, a_other, *group, store, kv)

    kv = jnp.zeros((NC * ABLK, TILE), F32)
    left, right, down, up, bounds, mine = lax.optimization_barrier((left, right, down, up, bounds, table_a))
    first_two = go(right, True, -1)
    a_other = lax.ppermute(mine, "core", swap)
    left_down, right_down = go(left, False, 1), go(right, False, 1)
    left_up, right_up = go(left, False, -1), go(right, False, -1)
    store, kv = build(0, (table_b, left, right, down, up), store, kv)
    first_two, right_down, down, kv = lax.optimization_barrier((first_two, right_down, down, kv))
    two_up, two_down, second_two = go(first_two, False, -1), go(first_two, False, 1), go(down, False, 1)
    right_two = go(right_down, False, 1)
    store, kv = build(5, (first_two, right_down), store, kv)
    left_up, right_up, left_down, kv = lax.optimization_barrier((left_up, right_up, left_down, kv))
    left_two = go(left_up, False, -1)
    store, kv = build(7, (left_up, right_up, left_down), store, kv)
    two_up, kv = lax.optimization_barrier((two_up, kv))
    both_two = go(two_up, False, -1)
    store, kv = build(10, (two_up, right_two, left_two), store, kv)
    second_two, two_down, both_two, kv = lax.optimization_barrier((second_two, two_down, both_two, kv))
    store, kv = build(13, (second_two, two_down, both_two), store, kv)

    def half(over_rows, parts, copies, store):
        last = copies == 0
        sums = jax.ShapeDtypeStruct((NCHIP, TILE // LANES, LANES) if last else (copies, NCHIP, TILE), F32)
        logs = jax.ShapeDtypeStruct((ABLK * TILE // LANES, LANES), F32)
        return pl.pallas_call(
            lambda *refs: pass_kernel(over_rows, last, *refs),
            out_shape=(sums, logs if last else pltpu.VMEM((CAP, TILE, TILE), BF16)),
            in_specs=[SM, SM, SM, VM, VM],
            out_specs=(VM, VM),
            scratch_shapes=[pltpu.VMEM((NCHIP, TILE), F32), pltpu.VMEM((NCHIP, TILE), F32)],
            input_output_aliases={} if last else {4: 1},
            compiler_params=params(),
            name="rows" if over_rows else "columns",
        )(pairs, bounds, place, parts, store)

    for step in range(ITERS):
        if step:
            kv, store = half(True, ktu_parts, NC * NZ, store)
        kv_parts = lax.all_to_all(kv, ("core", "z"), 0, 0, tiled=True)
        if step < ITERS - 1:
            ktu, store = half(False, kv_parts, NCHIP, store)
            ktu_parts = lax.all_to_all(ktu, ("y", "x"), 0, 0, tiled=True)
    ktu, log_u = half(False, kv_parts, 0, store)
    mine = lax.all_to_all(ktu, ("y", "x"), 0, 0, tiled=True)
    log_v = jnp.log(1.0 / (1.0 + jnp.sum(mine, axis=0)))
    return log_u.reshape(-1), log_v.reshape(-1)


def solution(mesh):
    fine = jax.sharding.Mesh(mesh.devices.reshape(NY, NX, NC, NZ), ("y", "x", "core", "z"))
    a_axes = ("y", "x", "core")
    b_axes = ("z", "y", "x", "core")
    in_specs = (P(a_axes, None), P(b_axes, None), P(a_axes, "z", None), P(a_axes, "z", None), P(a_axes, "z"))
    out_specs = (P(a_axes), P(b_axes))
    return jax.shard_map(on_device, mesh=fine, in_specs=in_specs, out_specs=out_specs, check_vma=False)
```

```python
import math

import jax
import jax.numpy as jnp
from jax import lax
from jax.experimental import pallas as pl
from jax.experimental.pallas import tpu as pltpu
from jax.sharding import PartitionSpec as P

TILE = 512
ABLK = 8
ITERS = 3
LANES = 128
BUILD_STEP = 2
BUFFERS = 4
ROW_STEP = 4
COLUMN_STEP = 8
NY, NX, NC, NZ = 4, 4, 2, 4
NCHIP = NY * NX
SLOTS = 32
CAP = NC * SLOTS
F32 = jnp.float32
BF16 = jnp.bfloat16
VM = pl.BlockSpec(memory_space=pltpu.VMEM)
SM = pl.BlockSpec(memory_space=pltpu.SMEM)
ANY = pl.BlockSpec(memory_space=pl.ANY)
HB = pl.BlockSpec(memory_space=pltpu.HBM)


ORDER = (
    ((0, 0), (3, 0), (1, 0), (0, 3), (0, 1)),
    ((2, 0), (1, 3)),
    ((3, 1), (1, 1), (3, 3)),
    ((2, 1), (1, 2)),
    ((3, 2), (0, 2), (2, 3)),
    ((2, 2),),
)


def plan_kernel(lists, place, table, pairs, bounds, tally):
    core, my_y, my_x = place[0], place[1], place[2]
    for k in range(NCHIP + 1):
        tally[k] = 0

    def scan(body):
        for which in range(NC):
            live = lists[which, 2 * SLOTS]

            def step(s, carry, which=which):
                b = lists[which, SLOTS + s]

                @pl.when((b % NC) == core)
                def _():
                    chip = b // NC
                    dy = (chip // NX - my_y + NY) % NY
                    dx = (chip % NX - my_x + NX) % NX
                    code = jnp.where(core == 0, dx * NY + dy, dy * NX + dx)
                    body(which * ABLK + lists[which, s], chip, table[code])

                return carry

            lax.fori_loop(0, jnp.minimum(live, SLOTS), step, 0)

    def count(a, chip, rank):
        tally[rank + 1] = tally[rank + 1] + 1

    scan(count)
    for k in range(NCHIP):
        tally[k + 1] = tally[k + 1] + tally[k]
    for k in range(NCHIP + 1):
        bounds[k] = tally[k]

    def put(a, chip, rank):
        spot = tally[rank]
        pairs[0, spot] = a
        pairs[1, spot] = chip
        pairs[2, spot] = rank
        tally[rank] = spot + 1

    scan(put)


def room_kernel(pairs, bounds, place, store):
    pass


def build_kernel(scale, first, blocks, last, pairs, bounds, place, a_mine, a_other, *refs):
    pieces = len(refs) - 9
    b_refs, (_, kv_in, store, out), scratch = refs[:pieces], refs[pieces : pieces + 4], refs[pieces + 4 :]
    kv, abuf, bbuf, a_sems, b_sems = scratch
    core = place[0]
    low, high = bounds[first], bounds[first + blocks]
    ahead = BUFFERS - BUILD_STEP

    def fetch(t):
        @pl.when(t < high)
        def _():
            a = pairs[0, t]
            slot = (t - low) % BUFFERS
            row = pl.multiple_of((a % ABLK) * TILE, TILE)

            @pl.when(a // ABLK == core)
            def _():
                pltpu.make_async_copy(a_mine.at[pl.ds(row, TILE)], abuf.at[slot], a_sems.at[slot]).start()

            @pl.when(a // ABLK != core)
            def _():
                pltpu.make_async_copy(a_other.at[pl.ds(row, TILE)], abuf.at[slot], a_sems.at[slot]).start()

    loads, filled = [], 0
    for k in range(pieces):
        rows = b_refs[k].shape[0]
        spot = bbuf.at[filled // TILE, pl.ds(filled % TILE, rows)]
        loads.append(pltpu.make_async_copy(b_refs[k], spot, b_sems.at[k]))
        filled += rows
    for load in loads:
        load.start()
    for k in range(ahead):
        fetch(low + k)
    kv[...] = kv_in[...]
    for load in loads:
        load.wait()

    def step(c, carry):
        base = low + c * BUILD_STEP
        for k in range(BUILD_STEP):
            fetch(base + ahead + k)
        for k in range(BUILD_STEP):

            @pl.when(base + k < high)
            def _(k=k):
                slot = (base + k - low) % BUFFERS
                pltpu.make_async_copy(a_mine.at[pl.ds(0, TILE)], abuf.at[slot], a_sems.at[slot]).wait()

        sums = []
        for k in range(BUILD_STEP):
            t = jnp.minimum(base + k, high - 1)
            block_a, block_b = abuf[(t - low) % BUFFERS], bbuf[pairs[2, t] - first]
            score = lax.dot_general(block_a, block_b, (((1,), (1,)), ((), ())), preferred_element_type=F32)
            tile = jnp.exp(score * scale).astype(BF16)
            store[t] = tile
            wide = tile.astype(F32)
            part = wide[:, :LANES]
            for q in range(1, TILE // LANES):
                part = part + wide[:, q * LANES : (q + 1) * LANES]
            part = jnp.sum(part.T, axis=0, keepdims=True)
            sums.append((pairs[0, t], jnp.where(base + k < high, part, 0.0)))
        for a, part in sums:
            kv[pl.ds(a, 1), :] += part
        return carry

    lax.fori_loop(0, (high - low + BUILD_STEP - 1) // BUILD_STEP, step, 0)
    if last:
        spread(out, kv[...])
    else:
        out[...] = kv[...]


def spread(out, value):
    for k in range(out.shape[0]):
        out[k] = value


def pass_kernel(over_rows, last, pairs, bounds, place, parts, store, out, *refs):
    sums, weight = refs[-2:]
    scaling = 1.0 / (1.0 + jnp.sum(parts[...], axis=0))
    weight[...] = scaling.astype(BF16).astype(F32)
    if last:
        logs = jnp.log(jnp.where(place[0] == 0, scaling[:ABLK], scaling[ABLK:]))
        for k in range(ABLK):
            for q in range(TILE // LANES):
                refs[0][pl.ds(k * (TILE // LANES) + q, 1), :] = logs[k : k + 1, q * LANES : (q + 1) * LANES]
    sums[...] = jnp.zeros_like(sums)
    number = bounds[NCHIP]
    size = ROW_STEP if over_rows else COLUMN_STEP
    dims = (((1,), (1,)), ((), ())) if over_rows else (((1,), (0,)), ((), ()))

    def step(c, carry):
        found = []
        for k in range(size):
            t = c * size + k
            safe = jnp.minimum(t, number - 1)
            a = pairs[0, safe]
            b = pairs[1, safe]
            source, target = (b, a) if over_rows else (a, b)
            row = jnp.where(t < number, weight[pl.ds(source, 1), :], 0.0)
            if over_rows and k % 2 == 0:
                part = store[safe, :, :LANES].astype(F32) * row[:, :LANES]
                for q in range(1, TILE // LANES):
                    lanes = slice(q * LANES, (q + 1) * LANES)
                    part = part + store[safe, :, lanes].astype(F32) * row[:, lanes]
                found.append((target, jnp.sum(part.T, axis=0, keepdims=True)))
                continue
            row = jnp.broadcast_to(row, (16, TILE)).astype(BF16)
            found.append((target, lax.dot_general(row, store[safe], dims, preferred_element_type=F32)[0:1]))
        for target, part in found:
            sums[pl.ds(target, 1), :] += part
        return carry

    lax.fori_loop(0, (number + size - 1) // size, step, 0)
    if last:
        for q in range(TILE // LANES):
            out[:, q, :] = sums[:, q * LANES : (q + 1) * LANES]
    else:
        spread(out, sums[...])


def params(mib=16):
    return pltpu.CompilerParams(vmem_limit_bytes=mib << 20)


def moves(first, shift):
    pairs = []
    for y in range(NY):
        for x in range(NX):
            for c in range(NC):
                dy, dx = (0, shift) if (c == 0) == first else (shift, 0)
                there = ((y + dy) % NY * NX + (x + dx) % NX) * NC + c
                pairs.append(((y * NX + x) * NC + c, there))
    return pairs


def go(block, first, shift):
    return lax.ppermute(block, ("y", "x", "core"), moves(first, shift))


def on_device(table_a, table_b, pair_a, pair_b, pair_count):
    width = table_a.shape[1]
    scale = 2.5 / math.sqrt(width)
    core = lax.axis_index("core")
    swap = [(0, 1), (1, 0)]
    own = jnp.concatenate(
        [pair_a.reshape(1, -1), pair_b.reshape(1, -1), pair_count.reshape(1, 1), jnp.zeros((1, 63), jnp.int32)], axis=1
    )
    a_other = lax.ppermute(table_a, "core", swap)
    other = lax.ppermute(own, "core", swap)
    lists = jnp.where(core == 0, jnp.concatenate([own, other]), jnp.concatenate([other, own]))
    place = jnp.stack([core, lax.axis_index("y"), lax.axis_index("x")]).astype(jnp.int32)
    table = [0] * NCHIP
    for rank, (f, s) in enumerate(sum(ORDER, ())):
        table[f * NY + s] = rank
    left, right = go(table_b, True, 1), go(table_b, True, -1)
    down, up = go(table_b, False, 1), go(table_b, False, -1)

    pairs, bounds = pl.pallas_call(
        plan_kernel,
        out_shape=(jax.ShapeDtypeStruct((3, CAP), jnp.int32), jax.ShapeDtypeStruct((NCHIP + 1,), jnp.int32)),
        in_specs=[SM, SM, SM],
        out_specs=(SM, SM),
        scratch_shapes=[pltpu.SMEM((NCHIP + 1,), jnp.int32)],
        compiler_params=params(1),
        name="plan",
    )(lists, place, jnp.array(table, jnp.int32))

    store = pl.pallas_call(
        room_kernel,
        out_shape=pltpu.VMEM((CAP, TILE, TILE), BF16),
        in_specs=[SM, SM, SM],
        out_specs=VM,
        compiler_params=params(),
        name="room",
    )(pairs, bounds, place)

    def build(first, group, store, kv):
        blocks = sum(piece.shape[0] for piece in group) // TILE
        pieces = len(group)
        last = first + blocks == NCHIP
        shape = (NC * NZ, NC * ABLK, TILE) if last else (NC * ABLK, TILE)
        share = 2 * blocks
        return pl.pallas_call(
            lambda *refs: build_kernel(scale, first, blocks, last, *refs),
            out_shape=(pltpu.VMEM((CAP, TILE, TILE), BF16), jax.ShapeDtypeStruct(shape, F32)),
            in_specs=[SM, SM, SM, HB, HB] + [ANY] * pieces + [VM, VM],
            out_specs=(VM, VM),
            scratch_shapes=[
                pltpu.VMEM((NC * ABLK, TILE), F32),
                pltpu.VMEM((BUFFERS, TILE, width), BF16),
                pltpu.VMEM((blocks, TILE, width), BF16),
                pltpu.SemaphoreType.DMA((BUFFERS,)),
                pltpu.SemaphoreType.DMA((pieces,)),
            ],
            input_output_aliases={5 + pieces: 0},
            cost_estimate=pl.CostEstimate(
                flops=share * 2 * TILE * TILE * width,
                transcendentals=share * TILE * TILE,
                bytes_accessed=share * 2 * TILE * width * 2,
            ),
            compiler_params=params(),
            name="build",
        )(pairs, bounds, place, table_a, a_other, *group, store, kv)

    kv = jnp.zeros((NC * ABLK, TILE), F32)
    left, right, bounds = lax.optimization_barrier((left, right, bounds))
    first_two = go(right, True, -1)
    left_down, right_down = go(left, False, 1), go(right, False, 1)
    left_up, right_up = go(left, False, -1), go(right, False, -1)
    store, kv = build(0, (table_b, left, right, down, up), store, kv)
    first_two, right_down, down, kv = lax.optimization_barrier((first_two, right_down, down, kv))
    two_up, two_down, second_two = go(first_two, False, -1), go(first_two, False, 1), go(down, False, 1)
    right_two = go(right_down, False, 1)
    store, kv = build(5, (first_two, right_down), store, kv)
    left_up, right_up, left_down, kv = lax.optimization_barrier((left_up, right_up, left_down, kv))
    left_two = go(left_up, False, -1)
    store, kv = build(7, (left_up, right_up, left_down), store, kv)
    two_up, kv = lax.optimization_barrier((two_up, kv))
    both_two = go(two_up, False, -1)
    store, kv = build(10, (two_up, right_two), store, kv)
    left_two, second_two, two_down, kv = lax.optimization_barrier((left_two, second_two, two_down, kv))
    store, kv = build(12, (left_two, second_two, two_down), store, kv)
    both_two, kv = lax.optimization_barrier((both_two, kv))
    store, kv = build(15, (both_two,), store, kv)

    def half(over_rows, parts, copies, store):
        last = copies == 0
        sums = jax.ShapeDtypeStruct((NCHIP, TILE // LANES, LANES) if last else (copies, NCHIP, TILE), F32)
        logs = jax.ShapeDtypeStruct((ABLK * TILE // LANES, LANES), F32)
        return pl.pallas_call(
            lambda *refs: pass_kernel(over_rows, last, *refs),
            out_shape=(sums, logs if last else pltpu.VMEM((CAP, TILE, TILE), BF16)),
            in_specs=[SM, SM, SM, VM, VM],
            out_specs=(VM, VM),
            scratch_shapes=[pltpu.VMEM((NCHIP, TILE), F32), pltpu.VMEM((NCHIP, TILE), F32)],
            input_output_aliases={} if last else {4: 1},
            compiler_params=params(),
            name="rows" if over_rows else "columns",
        )(pairs, bounds, place, parts, store)

    for step in range(ITERS):
        if step:
            kv, store = half(True, ktu_parts, NC * NZ, store)
        kv_parts = lax.all_to_all(kv, ("core", "z"), 0, 0, tiled=True)
        if step < ITERS - 1:
            ktu, store = half(False, kv_parts, NCHIP, store)
            ktu_parts = lax.all_to_all(ktu, ("y", "x"), 0, 0, tiled=True)
    ktu, log_u = half(False, kv_parts, 0, store)
    mine = lax.all_to_all(ktu, ("y", "x"), 0, 0, tiled=True)
    log_v = jnp.log(1.0 / (1.0 + jnp.sum(mine, axis=0)))
    return log_u.reshape(-1), log_v.reshape(-1)


def solution(mesh):
    fine = jax.sharding.Mesh(mesh.devices.reshape(NY, NX, NC, NZ), ("y", "x", "core", "z"))
    a_axes = ("y", "x", "core")
    b_axes = ("z", "y", "x", "core")
    in_specs = (P(a_axes, None), P(b_axes, None), P(a_axes, "z", None), P(a_axes, "z", None), P(a_axes, "z"))
    out_specs = (P(a_axes), P(b_axes))
    return jax.shard_map(on_device, mesh=fine, in_specs=in_specs, out_specs=out_specs, check_vma=False)
```

```python
import math

import jax
import jax.numpy as jnp
from jax import lax
from jax.experimental import pallas as pl
from jax.experimental.pallas import tpu as pltpu
from jax.sharding import PartitionSpec as P

TILE = 512
ABLK = 8
ITERS = 3
LANES = 128
BUILD_STEP = 2
BUFFERS = 4
ROW_STEP = 8
COLUMN_STEP = 8
NY, NX, NC, NZ = 4, 4, 2, 4
NCHIP = NY * NX
SLOTS = 32
CAP = NC * SLOTS
F32 = jnp.float32
BF16 = jnp.bfloat16
VM = pl.BlockSpec(memory_space=pltpu.VMEM)
SM = pl.BlockSpec(memory_space=pltpu.SMEM)
ANY = pl.BlockSpec(memory_space=pl.ANY)
HB = pl.BlockSpec(memory_space=pltpu.HBM)


ORDER = (
    ((0, 0), (3, 0), (1, 0), (0, 3), (0, 1)),
    ((2, 0), (1, 3)),
    ((3, 1), (1, 1), (3, 3)),
    ((2, 1), (1, 2)),
    ((3, 2), (0, 2), (2, 3)),
    ((2, 2),),
)


def plan_kernel(lists, place, table, pairs, bounds, tally):
    core, my_y, my_x = place[0], place[1], place[2]
    for k in range(NCHIP + 1):
        tally[k] = 0

    def scan(body):
        for which in range(NC):
            live = lists[which, 2 * SLOTS]

            def step(s, carry, which=which):
                b = lists[which, SLOTS + s]

                @pl.when((b % NC) == core)
                def _():
                    chip = b // NC
                    dy = (chip // NX - my_y + NY) % NY
                    dx = (chip % NX - my_x + NX) % NX
                    code = jnp.where(core == 0, dx * NY + dy, dy * NX + dx)
                    body(which * ABLK + lists[which, s], chip, table[code])

                return carry

            lax.fori_loop(0, jnp.minimum(live, SLOTS), step, 0)

    def count(a, chip, rank):
        tally[rank + 1] = tally[rank + 1] + 1

    scan(count)
    for k in range(NCHIP):
        tally[k + 1] = tally[k + 1] + tally[k]
    for k in range(NCHIP + 1):
        bounds[k] = tally[k]

    def put(a, chip, rank):
        spot = tally[rank]
        pairs[0, spot] = a
        pairs[1, spot] = chip
        pairs[2, spot] = rank
        tally[rank] = spot + 1

    scan(put)


def room_kernel(pairs, bounds, place, store):
    pass


def build_kernel(scale, first, blocks, last, pairs, bounds, place, a_mine, a_other, *refs):
    pieces = len(refs) - 9
    b_refs, (_, kv_in, store, out), scratch = refs[:pieces], refs[pieces : pieces + 4], refs[pieces + 4 :]
    kv, abuf, bbuf, a_sems, b_sems = scratch
    core = place[0]
    low, high = bounds[first], bounds[first + blocks]
    ahead = BUFFERS - BUILD_STEP

    def fetch(t):
        @pl.when(t < high)
        def _():
            a = pairs[0, t]
            slot = (t - low) % BUFFERS
            row = pl.multiple_of((a % ABLK) * TILE, TILE)

            @pl.when(a // ABLK == core)
            def _():
                pltpu.make_async_copy(a_mine.at[pl.ds(row, TILE)], abuf.at[slot], a_sems.at[slot]).start()

            @pl.when(a // ABLK != core)
            def _():
                pltpu.make_async_copy(a_other.at[pl.ds(row, TILE)], abuf.at[slot], a_sems.at[slot]).start()

    loads, filled = [], 0
    for k in range(pieces):
        rows = b_refs[k].shape[0]
        spot = bbuf.at[filled // TILE, pl.ds(filled % TILE, rows)]
        loads.append(pltpu.make_async_copy(b_refs[k], spot, b_sems.at[k]))
        filled += rows
    for load in loads:
        load.start()
    for k in range(ahead):
        fetch(low + k)
    kv[...] = kv_in[...]
    for load in loads:
        load.wait()

    def step(c, carry):
        base = low + c * BUILD_STEP
        for k in range(BUILD_STEP):
            fetch(base + ahead + k)
        for k in range(BUILD_STEP):

            @pl.when(base + k < high)
            def _(k=k):
                slot = (base + k - low) % BUFFERS
                pltpu.make_async_copy(a_mine.at[pl.ds(0, TILE)], abuf.at[slot], a_sems.at[slot]).wait()

        sums = []
        for k in range(BUILD_STEP):
            t = jnp.minimum(base + k, high - 1)
            block_a, block_b = abuf[(t - low) % BUFFERS], bbuf[pairs[2, t] - first]
            score = lax.dot_general(block_a, block_b, (((1,), (1,)), ((), ())), preferred_element_type=F32)
            tile = jnp.exp(score * scale).astype(BF16)
            store[t] = tile
            wide = tile.astype(F32)
            part = wide[:, :LANES]
            for q in range(1, TILE // LANES):
                part = part + wide[:, q * LANES : (q + 1) * LANES]
            part = jnp.sum(part.T, axis=0, keepdims=True)
            sums.append((pairs[0, t], jnp.where(base + k < high, part, 0.0)))
        for a, part in sums:
            kv[pl.ds(a, 1), :] += part
        return carry

    lax.fori_loop(0, (high - low + BUILD_STEP - 1) // BUILD_STEP, step, 0)
    if last:
        spread(out, kv[...])
    else:
        out[...] = kv[...]


def spread(out, value):
    for k in range(out.shape[0]):
        out[k] = value


def pass_kernel(over_rows, last, pairs, bounds, place, parts, store, out, *refs):
    sums, weight = refs[-2:]
    scaling = 1.0 / (1.0 + jnp.sum(parts[...], axis=0))
    weight[...] = scaling.astype(BF16).astype(F32)
    if last:
        logs = jnp.log(jnp.where(place[0] == 0, scaling[:ABLK], scaling[ABLK:]))
        for k in range(ABLK):
            for q in range(TILE // LANES):
                refs[0][pl.ds(k * (TILE // LANES) + q, 1), :] = logs[k : k + 1, q * LANES : (q + 1) * LANES]
    sums[...] = jnp.zeros_like(sums)
    number = bounds[NCHIP]
    size = ROW_STEP if over_rows else COLUMN_STEP
    dims = (((1,), (1,)), ((), ())) if over_rows else (((1,), (0,)), ((), ()))

    def step(c, carry):
        found = []
        for k in range(size):
            t = c * size + k
            safe = jnp.minimum(t, number - 1)
            a = pairs[0, safe]
            b = pairs[1, safe]
            source, target = (b, a) if over_rows else (a, b)
            row = jnp.where(t < number, weight[pl.ds(source, 1), :], 0.0)
            if over_rows and k % 2 == 0:
                part = store[safe, :, :LANES].astype(F32) * row[:, :LANES]
                for q in range(1, TILE // LANES):
                    lanes = slice(q * LANES, (q + 1) * LANES)
                    part = part + store[safe, :, lanes].astype(F32) * row[:, lanes]
                found.append((target, jnp.sum(part.T, axis=0, keepdims=True)))
                continue
            if not over_rows and k % 4 == 0:
                tall = jnp.broadcast_to(row, (LANES, TILE)).T
                cut = []
                for q in range(TILE // LANES):
                    lanes = slice(q * LANES, (q + 1) * LANES)
                    cut.append(jnp.sum(store[safe, :, lanes].astype(F32) * tall, axis=0, keepdims=True))
                found.append((target, jnp.concatenate(cut, axis=1)))
                continue
            row = jnp.broadcast_to(row, (16, TILE)).astype(BF16)
            found.append((target, lax.dot_general(row, store[safe], dims, preferred_element_type=F32)[0:1]))
        for target, part in found:
            sums[pl.ds(target, 1), :] += part
        return carry

    lax.fori_loop(0, (number + size - 1) // size, step, 0)
    if last:
        for q in range(TILE // LANES):
            out[:, q, :] = sums[:, q * LANES : (q + 1) * LANES]
    else:
        spread(out, sums[...])


def params(mib=16):
    return pltpu.CompilerParams(vmem_limit_bytes=mib << 20)


def moves(first, shift):
    pairs = []
    for y in range(NY):
        for x in range(NX):
            for c in range(NC):
                dy, dx = (0, shift) if (c == 0) == first else (shift, 0)
                there = ((y + dy) % NY * NX + (x + dx) % NX) * NC + c
                pairs.append(((y * NX + x) * NC + c, there))
    return pairs


def go(block, first, shift):
    return lax.ppermute(block, ("y", "x", "core"), moves(first, shift))


def on_device(table_a, table_b, pair_a, pair_b, pair_count):
    width = table_a.shape[1]
    scale = 2.5 / math.sqrt(width)
    core = lax.axis_index("core")
    swap = [(0, 1), (1, 0)]
    own = jnp.concatenate(
        [pair_a.reshape(1, -1), pair_b.reshape(1, -1), pair_count.reshape(1, 1), jnp.zeros((1, 63), jnp.int32)], axis=1
    )
    a_other = lax.ppermute(table_a, "core", swap)
    other = lax.ppermute(own, "core", swap)
    lists = jnp.where(core == 0, jnp.concatenate([own, other]), jnp.concatenate([other, own]))
    place = jnp.stack([core, lax.axis_index("y"), lax.axis_index("x")]).astype(jnp.int32)
    table = [0] * NCHIP
    for rank, (f, s) in enumerate(sum(ORDER, ())):
        table[f * NY + s] = rank
    left, right = go(table_b, True, 1), go(table_b, True, -1)
    down, up = go(table_b, False, 1), go(table_b, False, -1)

    pairs, bounds = pl.pallas_call(
        plan_kernel,
        out_shape=(jax.ShapeDtypeStruct((3, CAP), jnp.int32), jax.ShapeDtypeStruct((NCHIP + 1,), jnp.int32)),
        in_specs=[SM, SM, SM],
        out_specs=(SM, SM),
        scratch_shapes=[pltpu.SMEM((NCHIP + 1,), jnp.int32)],
        compiler_params=params(1),
        name="plan",
    )(lists, place, jnp.array(table, jnp.int32))

    store = pl.pallas_call(
        room_kernel,
        out_shape=pltpu.VMEM((CAP, TILE, TILE), BF16),
        in_specs=[SM, SM, SM],
        out_specs=VM,
        compiler_params=params(),
        name="room",
    )(pairs, bounds, place)

    def build(first, group, store, kv):
        blocks = sum(piece.shape[0] for piece in group) // TILE
        pieces = len(group)
        last = first + blocks == NCHIP
        shape = (NC * NZ, NC * ABLK, TILE) if last else (NC * ABLK, TILE)
        share = 2 * blocks
        return pl.pallas_call(
            lambda *refs: build_kernel(scale, first, blocks, last, *refs),
            out_shape=(pltpu.VMEM((CAP, TILE, TILE), BF16), jax.ShapeDtypeStruct(shape, F32)),
            in_specs=[SM, SM, SM, HB, HB] + [ANY] * pieces + [VM, VM],
            out_specs=(VM, VM),
            scratch_shapes=[
                pltpu.VMEM((NC * ABLK, TILE), F32),
                pltpu.VMEM((BUFFERS, TILE, width), BF16),
                pltpu.VMEM((blocks, TILE, width), BF16),
                pltpu.SemaphoreType.DMA((BUFFERS,)),
                pltpu.SemaphoreType.DMA((pieces,)),
            ],
            input_output_aliases={5 + pieces: 0},
            cost_estimate=pl.CostEstimate(
                flops=share * 2 * TILE * TILE * width,
                transcendentals=share * TILE * TILE,
                bytes_accessed=share * 2 * TILE * width * 2,
            ),
            compiler_params=params(),
            name="build",
        )(pairs, bounds, place, table_a, a_other, *group, store, kv)

    kv = jnp.zeros((NC * ABLK, TILE), F32)
    left, right, bounds = lax.optimization_barrier((left, right, bounds))
    first_two = go(right, True, -1)
    left_down, right_down = go(left, False, 1), go(right, False, 1)
    left_up, right_up = go(left, False, -1), go(right, False, -1)
    store, kv = build(0, (table_b, left, right, down, up), store, kv)
    first_two, right_down, down, kv = lax.optimization_barrier((first_two, right_down, down, kv))
    two_up, two_down, second_two = go(first_two, False, -1), go(first_two, False, 1), go(down, False, 1)
    right_two = go(right_down, False, 1)
    store, kv = build(5, (first_two, right_down), store, kv)
    left_up, right_up, left_down, kv = lax.optimization_barrier((left_up, right_up, left_down, kv))
    left_two = go(left_up, False, -1)
    store, kv = build(7, (left_up, right_up, left_down), store, kv)
    two_up, kv = lax.optimization_barrier((two_up, kv))
    both_two = go(two_up, False, -1)
    store, kv = build(10, (two_up, right_two), store, kv)
    left_two, second_two, two_down, kv = lax.optimization_barrier((left_two, second_two, two_down, kv))
    store, kv = build(12, (left_two, second_two, two_down), store, kv)
    both_two, kv = lax.optimization_barrier((both_two, kv))
    store, kv = build(15, (both_two,), store, kv)

    def half(over_rows, parts, copies, store):
        last = copies == 0
        sums = jax.ShapeDtypeStruct((NCHIP, TILE // LANES, LANES) if last else (copies, NCHIP, TILE), F32)
        logs = jax.ShapeDtypeStruct((ABLK * TILE // LANES, LANES), F32)
        return pl.pallas_call(
            lambda *refs: pass_kernel(over_rows, last, *refs),
            out_shape=(sums, logs if last else pltpu.VMEM((CAP, TILE, TILE), BF16)),
            in_specs=[SM, SM, SM, VM, VM],
            out_specs=(VM, VM),
            scratch_shapes=[pltpu.VMEM((NCHIP, TILE), F32), pltpu.VMEM((NCHIP, TILE), F32)],
            input_output_aliases={} if last else {4: 1},
            compiler_params=params(),
            name="rows" if over_rows else "columns",
        )(pairs, bounds, place, parts, store)

    for step in range(ITERS):
        if step:
            kv, store = half(True, ktu_parts, NC * NZ, store)
        kv_parts = lax.all_to_all(kv, ("core", "z"), 0, 0, tiled=True)
        if step < ITERS - 1:
            ktu, store = half(False, kv_parts, NCHIP, store)
            ktu_parts = lax.all_to_all(ktu, ("y", "x"), 0, 0, tiled=True)
    ktu, log_u = half(False, kv_parts, 0, store)
    mine = lax.all_to_all(ktu, ("y", "x"), 0, 0, tiled=True)
    log_v = jnp.log(1.0 / (1.0 + jnp.sum(mine, axis=0)))
    return log_u.reshape(-1), log_v.reshape(-1)


def solution(mesh):
    fine = jax.sharding.Mesh(mesh.devices.reshape(NY, NX, NC, NZ), ("y", "x", "core", "z"))
    a_axes = ("y", "x", "core")
    b_axes = ("z", "y", "x", "core")
    in_specs = (P(a_axes, None), P(b_axes, None), P(a_axes, "z", None), P(a_axes, "z", None), P(a_axes, "z"))
    out_specs = (P(a_axes), P(b_axes))
    return jax.shard_map(on_device, mesh=fine, in_specs=in_specs, out_specs=out_specs, check_vma=False)
```

```python
import math

import jax
import jax.numpy as jnp
from jax import lax
from jax.experimental import pallas as pl
from jax.experimental.pallas import tpu as pltpu
from jax.sharding import PartitionSpec as P

TILE = 512
ABLK = 8
ITERS = 3
LANES = 128
BUILD_STEP = 2
BUFFERS = 4
ROW_STEP = 8
COLUMN_STEP = 8
NY, NX, NC, NZ = 4, 4, 2, 4
NCHIP = NY * NX
SLOTS = 32
CAP = NC * SLOTS
F32 = jnp.float32
BF16 = jnp.bfloat16
VM = pl.BlockSpec(memory_space=pltpu.VMEM)
SM = pl.BlockSpec(memory_space=pltpu.SMEM)
ANY = pl.BlockSpec(memory_space=pl.ANY)
HB = pl.BlockSpec(memory_space=pltpu.HBM)


ORDER = (
    ((0, 0), (3, 0), (1, 0), (0, 3), (0, 1)),
    ((2, 0), (1, 3)),
    ((3, 1), (1, 1), (3, 3)),
    ((2, 1), (1, 2)),
    ((3, 2), (0, 2), (2, 3)),
    ((2, 2),),
)


def plan_kernel(lists, place, table, pairs, bounds, tally):
    core, my_y, my_x = place[0], place[1], place[2]
    for k in range(NCHIP + 1):
        tally[k] = 0

    def scan(body):
        for which in range(NC):
            live = lists[which, 2 * SLOTS]

            def step(s, carry, which=which):
                b = lists[which, SLOTS + s]

                @pl.when((b % NC) == core)
                def _():
                    chip = b // NC
                    dy = (chip // NX - my_y + NY) % NY
                    dx = (chip % NX - my_x + NX) % NX
                    code = jnp.where(core == 0, dx * NY + dy, dy * NX + dx)
                    body(which * ABLK + lists[which, s], chip, table[code])

                return carry

            lax.fori_loop(0, jnp.minimum(live, SLOTS), step, 0)

    def count(a, chip, rank):
        tally[rank + 1] = tally[rank + 1] + 1

    scan(count)
    for k in range(NCHIP):
        tally[k + 1] = tally[k + 1] + tally[k]
    for k in range(NCHIP + 1):
        bounds[k] = tally[k]

    def put(a, chip, rank):
        spot = tally[rank]
        pairs[0, spot] = a
        pairs[1, spot] = chip
        pairs[2, spot] = rank
        tally[rank] = spot + 1

    scan(put)


def room_kernel(pairs, bounds, place, store):
    pass


def build_kernel(scale, first, blocks, last, pairs, bounds, place, a_mine, a_other, *refs):
    pieces = len(refs) - 9
    b_refs, (_, kv_in, store, out), scratch = refs[:pieces], refs[pieces : pieces + 4], refs[pieces + 4 :]
    kv, abuf, bbuf, a_sems, b_sems = scratch
    core = place[0]
    low, high = bounds[first], bounds[first + blocks]
    ahead = BUFFERS - BUILD_STEP

    def fetch(t):
        @pl.when(t < high)
        def _():
            a = pairs[0, t]
            slot = (t - low) % BUFFERS
            row = pl.multiple_of((a % ABLK) * TILE, TILE)

            @pl.when(a // ABLK == core)
            def _():
                pltpu.make_async_copy(a_mine.at[pl.ds(row, TILE)], abuf.at[slot], a_sems.at[slot]).start()

            @pl.when(a // ABLK != core)
            def _():
                pltpu.make_async_copy(a_other.at[pl.ds(row, TILE)], abuf.at[slot], a_sems.at[slot]).start()

    loads, filled = [], 0
    for k in range(pieces):
        rows = b_refs[k].shape[0]
        spot = bbuf.at[filled // TILE, pl.ds(filled % TILE, rows)]
        loads.append(pltpu.make_async_copy(b_refs[k], spot, b_sems.at[k]))
        filled += rows
    for load in loads:
        load.start()
    for k in range(ahead):
        fetch(low + k)
    kv[...] = kv_in[...]
    for load in loads:
        load.wait()

    def step(c, carry):
        base = low + c * BUILD_STEP
        for k in range(BUILD_STEP):
            fetch(base + ahead + k)
        for k in range(BUILD_STEP):

            @pl.when(base + k < high)
            def _(k=k):
                slot = (base + k - low) % BUFFERS
                pltpu.make_async_copy(a_mine.at[pl.ds(0, TILE)], abuf.at[slot], a_sems.at[slot]).wait()

        sums = []
        for k in range(BUILD_STEP):
            t = jnp.minimum(base + k, high - 1)
            block_a, block_b = abuf[(t - low) % BUFFERS], bbuf[pairs[2, t] - first]
            score = lax.dot_general(block_a, block_b, (((1,), (1,)), ((), ())), preferred_element_type=F32)
            tile = jnp.exp(score * scale).astype(BF16)
            store[t] = tile
            wide = tile.astype(F32)
            part = wide[:, :LANES]
            for q in range(1, TILE // LANES):
                part = part + wide[:, q * LANES : (q + 1) * LANES]
            part = jnp.sum(part.T, axis=0, keepdims=True)
            sums.append((pairs[0, t], jnp.where(base + k < high, part, 0.0)))
        for a, part in sums:
            kv[pl.ds(a, 1), :] += part
        return carry

    lax.fori_loop(0, (high - low + BUILD_STEP - 1) // BUILD_STEP, step, 0)
    if last:
        spread(out, kv[...])
    else:
        out[...] = kv[...]


def spread(out, value):
    for k in range(out.shape[0]):
        out[k] = value


def pass_kernel(over_rows, last, pairs, bounds, place, parts, store, out, *refs):
    sums, weight = refs[-2:]
    scaling = 1.0 / (1.0 + jnp.sum(parts[...], axis=0))
    weight[...] = scaling.astype(BF16).astype(F32)
    if last:
        logs = jnp.log(jnp.where(place[0] == 0, scaling[:ABLK], scaling[ABLK:]))
        for k in range(ABLK):
            for q in range(TILE // LANES):
                refs[0][pl.ds(k * (TILE // LANES) + q, 1), :] = logs[k : k + 1, q * LANES : (q + 1) * LANES]
    sums[...] = jnp.zeros_like(sums)
    number = bounds[NCHIP]
    size = ROW_STEP if over_rows else COLUMN_STEP
    dims = (((1,), (1,)), ((), ())) if over_rows else (((1,), (0,)), ((), ()))

    def step(c, carry):
        found = []
        for k in range(size):
            t = c * size + k
            safe = jnp.minimum(t, number - 1)
            a = pairs[0, safe]
            b = pairs[1, safe]
            source, target = (b, a) if over_rows else (a, b)
            row = jnp.where(t < number, weight[pl.ds(source, 1), :], 0.0)
            if over_rows and k % 2 == 0:
                part = store[safe, :, :LANES].astype(F32) * row[:, :LANES]
                for q in range(1, TILE // LANES):
                    lanes = slice(q * LANES, (q + 1) * LANES)
                    part = part + store[safe, :, lanes].astype(F32) * row[:, lanes]
                found.append((target, jnp.sum(part.T, axis=0, keepdims=True)))
                continue
            if not over_rows and k % 3 == 0:
                tall = jnp.broadcast_to(row, (LANES, TILE)).T
                cut = []
                for q in range(TILE // LANES):
                    lanes = slice(q * LANES, (q + 1) * LANES)
                    cut.append(jnp.sum(store[safe, :, lanes].astype(F32) * tall, axis=0, keepdims=True))
                found.append((target, jnp.concatenate(cut, axis=1)))
                continue
            row = jnp.broadcast_to(row, (16, TILE)).astype(BF16)
            found.append((target, lax.dot_general(row, store[safe], dims, preferred_element_type=F32)[0:1]))
        for target, part in found:
            sums[pl.ds(target, 1), :] += part
        return carry

    lax.fori_loop(0, (number + size - 1) // size, step, 0)
    if last:
        for q in range(TILE // LANES):
            out[:, q, :] = sums[:, q * LANES : (q + 1) * LANES]
    else:
        spread(out, sums[...])


def params(mib=16):
    return pltpu.CompilerParams(vmem_limit_bytes=mib << 20)


def moves(first, shift):
    pairs = []
    for y in range(NY):
        for x in range(NX):
            for c in range(NC):
                dy, dx = (0, shift) if (c == 0) == first else (shift, 0)
                there = ((y + dy) % NY * NX + (x + dx) % NX) * NC + c
                pairs.append(((y * NX + x) * NC + c, there))
    return pairs


def go(block, first, shift):
    return lax.ppermute(block, ("y", "x", "core"), moves(first, shift))


def on_device(table_a, table_b, pair_a, pair_b, pair_count):
    width = table_a.shape[1]
    scale = 2.5 / math.sqrt(width)
    core = lax.axis_index("core")
    swap = [(0, 1), (1, 0)]
    own = jnp.concatenate(
        [pair_a.reshape(1, -1), pair_b.reshape(1, -1), pair_count.reshape(1, 1), jnp.zeros((1, 63), jnp.int32)], axis=1
    )
    a_other = lax.ppermute(table_a, "core", swap)
    other = lax.ppermute(own, "core", swap)
    lists = jnp.where(core == 0, jnp.concatenate([own, other]), jnp.concatenate([other, own]))
    place = jnp.stack([core, lax.axis_index("y"), lax.axis_index("x")]).astype(jnp.int32)
    table = [0] * NCHIP
    for rank, (f, s) in enumerate(sum(ORDER, ())):
        table[f * NY + s] = rank
    left, right = go(table_b, True, 1), go(table_b, True, -1)
    down, up = go(table_b, False, 1), go(table_b, False, -1)

    pairs, bounds = pl.pallas_call(
        plan_kernel,
        out_shape=(jax.ShapeDtypeStruct((3, CAP), jnp.int32), jax.ShapeDtypeStruct((NCHIP + 1,), jnp.int32)),
        in_specs=[SM, SM, SM],
        out_specs=(SM, SM),
        scratch_shapes=[pltpu.SMEM((NCHIP + 1,), jnp.int32)],
        compiler_params=params(1),
        name="plan",
    )(lists, place, jnp.array(table, jnp.int32))

    store = pl.pallas_call(
        room_kernel,
        out_shape=pltpu.VMEM((CAP, TILE, TILE), BF16),
        in_specs=[SM, SM, SM],
        out_specs=VM,
        compiler_params=params(),
        name="room",
    )(pairs, bounds, place)

    def build(first, group, store, kv):
        blocks = sum(piece.shape[0] for piece in group) // TILE
        pieces = len(group)
        last = first + blocks == NCHIP
        shape = (NC * NZ, NC * ABLK, TILE) if last else (NC * ABLK, TILE)
        share = 2 * blocks
        return pl.pallas_call(
            lambda *refs: build_kernel(scale, first, blocks, last, *refs),
            out_shape=(pltpu.VMEM((CAP, TILE, TILE), BF16), jax.ShapeDtypeStruct(shape, F32)),
            in_specs=[SM, SM, SM, HB, HB] + [ANY] * pieces + [VM, VM],
            out_specs=(VM, VM),
            scratch_shapes=[
                pltpu.VMEM((NC * ABLK, TILE), F32),
                pltpu.VMEM((BUFFERS, TILE, width), BF16),
                pltpu.VMEM((blocks, TILE, width), BF16),
                pltpu.SemaphoreType.DMA((BUFFERS,)),
                pltpu.SemaphoreType.DMA((pieces,)),
            ],
            input_output_aliases={5 + pieces: 0},
            cost_estimate=pl.CostEstimate(
                flops=share * 2 * TILE * TILE * width,
                transcendentals=share * TILE * TILE,
                bytes_accessed=share * 2 * TILE * width * 2,
            ),
            compiler_params=params(),
            name="build",
        )(pairs, bounds, place, table_a, a_other, *group, store, kv)

    kv = jnp.zeros((NC * ABLK, TILE), F32)
    left, right, bounds = lax.optimization_barrier((left, right, bounds))
    first_two = go(right, True, -1)
    left_down, right_down = go(left, False, 1), go(right, False, 1)
    left_up, right_up = go(left, False, -1), go(right, False, -1)
    store, kv = build(0, (table_b, left, right, down, up), store, kv)
    first_two, right_down, down, kv = lax.optimization_barrier((first_two, right_down, down, kv))
    two_up, two_down, second_two = go(first_two, False, -1), go(first_two, False, 1), go(down, False, 1)
    right_two = go(right_down, False, 1)
    store, kv = build(5, (first_two, right_down), store, kv)
    left_up, right_up, left_down, kv = lax.optimization_barrier((left_up, right_up, left_down, kv))
    left_two = go(left_up, False, -1)
    store, kv = build(7, (left_up, right_up, left_down), store, kv)
    two_up, kv = lax.optimization_barrier((two_up, kv))
    both_two = go(two_up, False, -1)
    store, kv = build(10, (two_up, right_two), store, kv)
    left_two, second_two, two_down, kv = lax.optimization_barrier((left_two, second_two, two_down, kv))
    store, kv = build(12, (left_two, second_two, two_down), store, kv)
    both_two, kv = lax.optimization_barrier((both_two, kv))
    store, kv = build(15, (both_two,), store, kv)

    def half(over_rows, parts, copies, store):
        last = copies == 0
        sums = jax.ShapeDtypeStruct((NCHIP, TILE // LANES, LANES) if last else (copies, NCHIP, TILE), F32)
        logs = jax.ShapeDtypeStruct((ABLK * TILE // LANES, LANES), F32)
        return pl.pallas_call(
            lambda *refs: pass_kernel(over_rows, last, *refs),
            out_shape=(sums, logs if last else pltpu.VMEM((CAP, TILE, TILE), BF16)),
            in_specs=[SM, SM, SM, VM, VM],
            out_specs=(VM, VM),
            scratch_shapes=[pltpu.VMEM((NCHIP, TILE), F32), pltpu.VMEM((NCHIP, TILE), F32)],
            input_output_aliases={} if last else {4: 1},
            compiler_params=params(),
            name="rows" if over_rows else "columns",
        )(pairs, bounds, place, parts, store)

    for step in range(ITERS):
        if step:
            kv, store = half(True, ktu_parts, NC * NZ, store)
        kv_parts = lax.all_to_all(kv, ("core", "z"), 0, 0, tiled=True)
        if step < ITERS - 1:
            ktu, store = half(False, kv_parts, NCHIP, store)
            ktu_parts = lax.all_to_all(ktu, ("y", "x"), 0, 0, tiled=True)
    ktu, log_u = half(False, kv_parts, 0, store)
    mine = lax.all_to_all(ktu, ("y", "x"), 0, 0, tiled=True)
    log_v = jnp.log(1.0 / (1.0 + jnp.sum(mine, axis=0)))
    return log_u.reshape(-1), log_v.reshape(-1)


def solution(mesh):
    fine = jax.sharding.Mesh(mesh.devices.reshape(NY, NX, NC, NZ), ("y", "x", "core", "z"))
    a_axes = ("y", "x", "core")
    b_axes = ("z", "y", "x", "core")
    in_specs = (P(a_axes, None), P(b_axes, None), P(a_axes, "z", None), P(a_axes, "z", None), P(a_axes, "z"))
    out_specs = (P(a_axes), P(b_axes))
    return jax.shard_map(on_device, mesh=fine, in_specs=in_specs, out_specs=out_specs, check_vma=False)
```

```python
import math

import jax
import jax.numpy as jnp
from jax import lax
from jax.experimental import pallas as pl
from jax.experimental.pallas import tpu as pltpu
from jax.sharding import PartitionSpec as P

TILE = 512
ABLK = 8
ITERS = 3
LANES = 128
BUILD_STEP = 2
BUFFERS = 4
ROW_STEP = 8
COLUMN_STEP = 8
NY, NX, NC, NZ = 4, 4, 2, 4
NCHIP = NY * NX
SLOTS = 32
CAP = NC * SLOTS
F32 = jnp.float32
BF16 = jnp.bfloat16
VM = pl.BlockSpec(memory_space=pltpu.VMEM)
SM = pl.BlockSpec(memory_space=pltpu.SMEM)
ANY = pl.BlockSpec(memory_space=pl.ANY)
HB = pl.BlockSpec(memory_space=pltpu.HBM)


ORDER = (
    ((0, 0), (3, 0), (1, 0), (0, 3), (0, 1)),
    ((2, 0), (1, 3)),
    ((3, 1), (1, 1), (3, 3)),
    ((2, 1), (1, 2)),
    ((3, 2), (0, 2), (2, 3)),
    ((2, 2),),
)


def plan_kernel(lists, place, table, pairs, bounds, tally):
    core, my_y, my_x = place[0], place[1], place[2]
    for k in range(NCHIP + 1):
        tally[k] = 0

    def scan(body):
        for which in range(NC):
            live = lists[which, 2 * SLOTS]

            def step(s, carry, which=which):
                b = lists[which, SLOTS + s]

                @pl.when((b % NC) == core)
                def _():
                    chip = b // NC
                    dy = (chip // NX - my_y + NY) % NY
                    dx = (chip % NX - my_x + NX) % NX
                    code = jnp.where(core == 0, dx * NY + dy, dy * NX + dx)
                    body(which * ABLK + lists[which, s], chip, table[code])

                return carry

            lax.fori_loop(0, jnp.minimum(live, SLOTS), step, 0)

    def count(a, chip, rank):
        tally[rank + 1] = tally[rank + 1] + 1

    scan(count)
    for k in range(NCHIP):
        tally[k + 1] = tally[k + 1] + tally[k]
    for k in range(NCHIP + 1):
        bounds[k] = tally[k]

    def put(a, chip, rank):
        spot = tally[rank]
        pairs[0, spot] = a
        pairs[1, spot] = chip
        pairs[2, spot] = rank
        tally[rank] = spot + 1

    scan(put)


def room_kernel(pairs, bounds, place, store):
    pass


def build_kernel(scale, first, blocks, last, pairs, bounds, place, a_mine, a_other, *refs):
    pieces = len(refs) - 9
    b_refs, (_, kv_in, store, out), scratch = refs[:pieces], refs[pieces : pieces + 4], refs[pieces + 4 :]
    kv, abuf, bbuf, a_sems, b_sems = scratch
    core = place[0]
    low, high = bounds[first], bounds[first + blocks]
    ahead = BUFFERS - BUILD_STEP

    def fetch(t):
        @pl.when(t < high)
        def _():
            a = pairs[0, t]
            slot = (t - low) % BUFFERS
            row = pl.multiple_of((a % ABLK) * TILE, TILE)

            @pl.when(a // ABLK == core)
            def _():
                pltpu.make_async_copy(a_mine.at[pl.ds(row, TILE)], abuf.at[slot], a_sems.at[slot]).start()

            @pl.when(a // ABLK != core)
            def _():
                pltpu.make_async_copy(a_other.at[pl.ds(row, TILE)], abuf.at[slot], a_sems.at[slot]).start()

    loads, filled = [], 0
    for k in range(pieces):
        rows = b_refs[k].shape[0]
        spot = bbuf.at[filled // TILE, pl.ds(filled % TILE, rows)]
        loads.append(pltpu.make_async_copy(b_refs[k], spot, b_sems.at[k]))
        filled += rows
    for load in loads:
        load.start()
    for k in range(ahead):
        fetch(low + k)
    kv[...] = kv_in[...]
    for load in loads:
        load.wait()

    def step(c, carry):
        base = low + c * BUILD_STEP
        for k in range(BUILD_STEP):
            fetch(base + ahead + k)
        for k in range(BUILD_STEP):

            @pl.when(base + k < high)
            def _(k=k):
                slot = (base + k - low) % BUFFERS
                pltpu.make_async_copy(a_mine.at[pl.ds(0, TILE)], abuf.at[slot], a_sems.at[slot]).wait()

        sums = []
        for k in range(BUILD_STEP):
            t = jnp.minimum(base + k, high - 1)
            block_a, block_b = abuf[(t - low) % BUFFERS], bbuf[pairs[2, t] - first]
            score = lax.dot_general(block_a, block_b, (((1,), (1,)), ((), ())), preferred_element_type=F32)
            tile = jnp.exp(score * scale).astype(BF16)
            store[t] = tile
            wide = tile.astype(F32)
            part = wide[:, :LANES]
            for q in range(1, TILE // LANES):
                part = part + wide[:, q * LANES : (q + 1) * LANES]
            part = jnp.sum(part.T, axis=0, keepdims=True)
            sums.append((pairs[0, t], jnp.where(base + k < high, part, 0.0)))
        for a, part in sums:
            kv[pl.ds(a, 1), :] += part
        return carry

    lax.fori_loop(0, (high - low + BUILD_STEP - 1) // BUILD_STEP, step, 0)
    if last:
        spread(out, kv[...])
    else:
        out[...] = kv[...]


def spread(out, value):
    for k in range(out.shape[0]):
        out[k] = value


def pass_kernel(over_rows, last, pairs, bounds, place, parts, store, out, *refs):
    sums, weight = refs[-2:]
    scaling = 1.0 / (1.0 + jnp.sum(parts[...], axis=0))
    weight[...] = scaling.astype(BF16).astype(F32)
    if last:
        logs = jnp.log(jnp.where(place[0] == 0, scaling[:ABLK], scaling[ABLK:]))
        for k in range(ABLK):
            for q in range(TILE // LANES):
                refs[0][pl.ds(k * (TILE // LANES) + q, 1), :] = logs[k : k + 1, q * LANES : (q + 1) * LANES]
    sums[...] = jnp.zeros_like(sums)
    number = bounds[NCHIP]
    size = ROW_STEP if over_rows else COLUMN_STEP
    dims = (((1,), (1,)), ((), ())) if over_rows else (((1,), (0,)), ((), ()))

    def step(c, carry):
        found = []
        for k in range(size):
            t = c * size + k
            safe = jnp.minimum(t, number - 1)
            a = pairs[0, safe]
            b = pairs[1, safe]
            source, target = (b, a) if over_rows else (a, b)
            row = jnp.where(t < number, weight[pl.ds(source, 1), :], 0.0)
            if over_rows and k % 2 == 0:
                part = store[safe, :, :LANES].astype(F32) * row[:, :LANES]
                for q in range(1, TILE // LANES):
                    lanes = slice(q * LANES, (q + 1) * LANES)
                    part = part + store[safe, :, lanes].astype(F32) * row[:, lanes]
                found.append((target, jnp.sum(part.T, axis=0, keepdims=True)))
                continue
            if not over_rows and k % 2 == 0:
                tall = jnp.broadcast_to(row, (LANES, TILE)).T
                cut = []
                for q in range(TILE // LANES):
                    lanes = slice(q * LANES, (q + 1) * LANES)
                    cut.append(jnp.sum(store[safe, :, lanes].astype(F32) * tall, axis=0, keepdims=True))
                found.append((target, jnp.concatenate(cut, axis=1)))
                continue
            row = jnp.broadcast_to(row, (16, TILE)).astype(BF16)
            found.append((target, lax.dot_general(row, store[safe], dims, preferred_element_type=F32)[0:1]))
        for target, part in found:
            sums[pl.ds(target, 1), :] += part
        return carry

    lax.fori_loop(0, (number + size - 1) // size, step, 0)
    if last:
        for q in range(TILE // LANES):
            out[:, q, :] = sums[:, q * LANES : (q + 1) * LANES]
    else:
        spread(out, sums[...])


def params(mib=16):
    return pltpu.CompilerParams(vmem_limit_bytes=mib << 20)


def moves(first, shift):
    pairs = []
    for y in range(NY):
        for x in range(NX):
            for c in range(NC):
                dy, dx = (0, shift) if (c == 0) == first else (shift, 0)
                there = ((y + dy) % NY * NX + (x + dx) % NX) * NC + c
                pairs.append(((y * NX + x) * NC + c, there))
    return pairs


def go(block, first, shift):
    return lax.ppermute(block, ("y", "x", "core"), moves(first, shift))


def on_device(table_a, table_b, pair_a, pair_b, pair_count):
    width = table_a.shape[1]
    scale = 2.5 / math.sqrt(width)
    core = lax.axis_index("core")
    swap = [(0, 1), (1, 0)]
    own = jnp.concatenate(
        [pair_a.reshape(1, -1), pair_b.reshape(1, -1), pair_count.reshape(1, 1), jnp.zeros((1, 63), jnp.int32)], axis=1
    )
    a_other = lax.ppermute(table_a, "core", swap)
    other = lax.ppermute(own, "core", swap)
    lists = jnp.where(core == 0, jnp.concatenate([own, other]), jnp.concatenate([other, own]))
    place = jnp.stack([core, lax.axis_index("y"), lax.axis_index("x")]).astype(jnp.int32)
    table = [0] * NCHIP
    for rank, (f, s) in enumerate(sum(ORDER, ())):
        table[f * NY + s] = rank
    left, right = go(table_b, True, 1), go(table_b, True, -1)
    down, up = go(table_b, False, 1), go(table_b, False, -1)

    pairs, bounds = pl.pallas_call(
        plan_kernel,
        out_shape=(jax.ShapeDtypeStruct((3, CAP), jnp.int32), jax.ShapeDtypeStruct((NCHIP + 1,), jnp.int32)),
        in_specs=[SM, SM, SM],
        out_specs=(SM, SM),
        scratch_shapes=[pltpu.SMEM((NCHIP + 1,), jnp.int32)],
        compiler_params=params(1),
        name="plan",
    )(lists, place, jnp.array(table, jnp.int32))

    store = pl.pallas_call(
        room_kernel,
        out_shape=pltpu.VMEM((CAP, TILE, TILE), BF16),
        in_specs=[SM, SM, SM],
        out_specs=VM,
        compiler_params=params(),
        name="room",
    )(pairs, bounds, place)

    def build(first, group, store, kv):
        blocks = sum(piece.shape[0] for piece in group) // TILE
        pieces = len(group)
        last = first + blocks == NCHIP
        shape = (NC * NZ, NC * ABLK, TILE) if last else (NC * ABLK, TILE)
        share = 2 * blocks
        return pl.pallas_call(
            lambda *refs: build_kernel(scale, first, blocks, last, *refs),
            out_shape=(pltpu.VMEM((CAP, TILE, TILE), BF16), jax.ShapeDtypeStruct(shape, F32)),
            in_specs=[SM, SM, SM, HB, HB] + [ANY] * pieces + [VM, VM],
            out_specs=(VM, VM),
            scratch_shapes=[
                pltpu.VMEM((NC * ABLK, TILE), F32),
                pltpu.VMEM((BUFFERS, TILE, width), BF16),
                pltpu.VMEM((blocks, TILE, width), BF16),
                pltpu.SemaphoreType.DMA((BUFFERS,)),
                pltpu.SemaphoreType.DMA((pieces,)),
            ],
            input_output_aliases={5 + pieces: 0},
            cost_estimate=pl.CostEstimate(
                flops=share * 2 * TILE * TILE * width,
                transcendentals=share * TILE * TILE,
                bytes_accessed=share * 2 * TILE * width * 2,
            ),
            compiler_params=params(),
            name="build",
        )(pairs, bounds, place, table_a, a_other, *group, store, kv)

    kv = jnp.zeros((NC * ABLK, TILE), F32)
    left, right, bounds = lax.optimization_barrier((left, right, bounds))
    first_two = go(right, True, -1)
    left_down, right_down = go(left, False, 1), go(right, False, 1)
    left_up, right_up = go(left, False, -1), go(right, False, -1)
    store, kv = build(0, (table_b, left, right, down, up), store, kv)
    first_two, right_down, down, kv = lax.optimization_barrier((first_two, right_down, down, kv))
    two_up, two_down, second_two = go(first_two, False, -1), go(first_two, False, 1), go(down, False, 1)
    right_two = go(right_down, False, 1)
    store, kv = build(5, (first_two, right_down), store, kv)
    left_up, right_up, left_down, kv = lax.optimization_barrier((left_up, right_up, left_down, kv))
    left_two = go(left_up, False, -1)
    store, kv = build(7, (left_up, right_up, left_down), store, kv)
    two_up, kv = lax.optimization_barrier((two_up, kv))
    both_two = go(two_up, False, -1)
    store, kv = build(10, (two_up, right_two), store, kv)
    left_two, second_two, two_down, kv = lax.optimization_barrier((left_two, second_two, two_down, kv))
    store, kv = build(12, (left_two, second_two, two_down), store, kv)
    both_two, kv = lax.optimization_barrier((both_two, kv))
    store, kv = build(15, (both_two,), store, kv)

    def half(over_rows, parts, copies, store):
        last = copies == 0
        sums = jax.ShapeDtypeStruct((NCHIP, TILE // LANES, LANES) if last else (copies, NCHIP, TILE), F32)
        logs = jax.ShapeDtypeStruct((ABLK * TILE // LANES, LANES), F32)
        return pl.pallas_call(
            lambda *refs: pass_kernel(over_rows, last, *refs),
            out_shape=(sums, logs if last else pltpu.VMEM((CAP, TILE, TILE), BF16)),
            in_specs=[SM, SM, SM, VM, VM],
            out_specs=(VM, VM),
            scratch_shapes=[pltpu.VMEM((NCHIP, TILE), F32), pltpu.VMEM((NCHIP, TILE), F32)],
            input_output_aliases={} if last else {4: 1},
            compiler_params=params(),
            name="rows" if over_rows else "columns",
        )(pairs, bounds, place, parts, store)

    for step in range(ITERS):
        if step:
            kv, store = half(True, ktu_parts, NC * NZ, store)
        kv_parts = lax.all_to_all(kv, ("core", "z"), 0, 0, tiled=True)
        if step < ITERS - 1:
            ktu, store = half(False, kv_parts, NCHIP, store)
            ktu_parts = lax.all_to_all(ktu, ("y", "x"), 0, 0, tiled=True)
    ktu, log_u = half(False, kv_parts, 0, store)
    mine = lax.all_to_all(ktu, ("y", "x"), 0, 0, tiled=True)
    log_v = jnp.log(1.0 / (1.0 + jnp.sum(mine, axis=0)))
    return log_u.reshape(-1), log_v.reshape(-1)


def solution(mesh):
    fine = jax.sharding.Mesh(mesh.devices.reshape(NY, NX, NC, NZ), ("y", "x", "core", "z"))
    a_axes = ("y", "x", "core")
    b_axes = ("z", "y", "x", "core")
    in_specs = (P(a_axes, None), P(b_axes, None), P(a_axes, "z", None), P(a_axes, "z", None), P(a_axes, "z"))
    out_specs = (P(a_axes), P(b_axes))
    return jax.shard_map(on_device, mesh=fine, in_specs=in_specs, out_specs=out_specs, check_vma=False)
```
